256 devices in a mesh: segment: 32 (over z_hi, y, x), tp: 8 (over z_lo, core).
Axes of the slice: x: 4, y: 4, z: 8 (z_hi: 2, z_lo: 4; z = z_hi * 4 + z_lo), core: 2. Of those that a mesh axis runs over, the one named last changes fastest.
Arguments:
- layer_input: bfloat16 [16384, 1024], P('segment'), may hold values from -6 to 6
- cotangent: bfloat16 [16384, 1024], P('segment'), may hold values from -6 to 6
- norm_gain: float32 [32, 1024], P('segment'), may hold values from 0.5 to 1.5
- qkv_weight: bfloat16 [32, 3, 1024, 1024], P('segment', None, None, 'tp'), may hold values from -0.1875 to 0.1875
- out_weight: bfloat16 [32, 1024, 1024], P('segment', 'tp'), may hold values from -0.1875 to 0.1875
- up_weight: bfloat16 [32, 1024, 4096], P('segment', None, 'tp'), may hold values from -0.1875 to 0.1875
- down_weight: bfloat16 [32, 4096, 1024], P('segment', 'tp'), may hold values from -0.09375 to 0.09375
- logit_scale: float32 [32, 16], P('segment', 'tp'), may hold values from 4 to 16
- neighbour_table: int32 [32, 4, 4], replicated, may hold values from 0 to 3, as said below
- valid_table: int32 [32, 4, 4], replicated, may hold values from 0 to 1
- patch_of_segment: int32 [32], P('segment'), may hold values from 0 to 31, each once
Outputs:
- received: bfloat16 [16384, 1024], P('segment')
- grad_qkv: bfloat16 [32, 3, 1024, 1024], P('segment', None, None, 'tp')
- grad_out: bfloat16 [32, 1024, 1024], P('segment', 'tp')
- grad_up: bfloat16 [32, 1024, 4096], P('segment', None, 'tp')
- grad_down: bfloat16 [32, 4096, 1024], P('segment', 'tp')
- grad_gain: float32 [32, 1024], P('segment')
- grad_scale: float32 [32, 16], P('segment', 'tp')
The draws below stay inside these ranges and needn't reach their ends.
Inputs may be any that keep to these rules, and one draw needn't show every extreme that they name: `neighbour_table`: in every patch, slot 0 of block b names b itself; the other slots of a block name distinct other blocks of the same patch. `patch_of_segment`: each segment works on a different patch.
All inputs are finite; a program needn't handle non-finite values.
Results may differ from the reference program's by a relative error of at most 0.013.
Values may be sent and summed in bfloat16 or wider, within the bound.
A program may use at most 64 MiB of HBM per device.

```python
import math
import jax
import jax.numpy as jnp
from jax import lax

D = 1024
H = 16
DH = 64
FF = 4096
BLK = 128
NEIGHBOUR_SLOTS = 4
TOK = 512
PATCH_BLOCKS = 4
TOKENS = 16384
N_SEGMENT = 32
N_TP = 8


def draw_neighbour_table(key, part):
    scores = jax.random.randint(key, (N_SEGMENT, PATCH_BLOCKS, PATCH_BLOCKS - 1), 0, 1 << 20) * PATCH_BLOCKS + jnp.arange(PATCH_BLOCKS - 1, dtype=jnp.int32)
    slot_ranking = jnp.argsort(scores, axis=-1, stable=True).astype(jnp.int32)
    block_offsets = slot_ranking[:, :, :NEIGHBOUR_SLOTS - 1] + 1
    block_ids = jnp.arange(PATCH_BLOCKS, dtype=jnp.int32)
    other_slots = (block_ids[None, :, None] + block_offsets) % PATCH_BLOCKS
    self_slot = jnp.broadcast_to(block_ids[None, :, None], (N_SEGMENT, PATCH_BLOCKS, 1))
    return jnp.concatenate([self_slot, other_slots], axis=-1).astype(jnp.int32)


def draw_valid_table(key, part):
    surplus_slots = jax.random.randint(key, (N_SEGMENT, PATCH_BLOCKS), 0, NEIGHBOUR_SLOTS)
    polar = (jnp.arange(N_SEGMENT, dtype=jnp.int32) % 4 == 0)[:, None]
    surplus_slots = jnp.where(polar, surplus_slots // 2, surplus_slots)
    slot_index_list = jnp.arange(NEIGHBOUR_SLOTS, dtype=jnp.int32)
    return (slot_index_list[None, None, :] <= surplus_slots[:, :, None]).astype(jnp.int32)


def block_levels(stream_key, extent, split, low, largest):
    level = 1.0
    for position, shards_of in split:
        steps = jax.random.uniform(jax.random.fold_in(jax.random.fold_in(stream_key, 6), position), (shards_of,), jnp.float32, low / len(split), largest / len(split))
        level = level * jnp.repeat(jnp.exp(steps), extent[position] // shards_of).reshape((-1,) + (1,) * (len(extent) - 1 - position))
    return level


def noise(stream_key, dims, scale, bound, split=(), held_as=jnp.bfloat16):
    values = scale * jax.random.normal(stream_key, dims, jnp.float32)
    if split:
        values = values * block_levels(stream_key, dims, split, -0.22, 0.18)
    return jnp.clip(values, -bound, bound).astype(held_as)


def setup_inputs(seed: int = 0) -> dict:
    splits = jax.random.split(jax.random.key(seed), 12)
    layer_input = noise(splits[0], (TOKENS, D), 1.0, 6.0, ((0, 32),))
    cotangent = noise(splits[1], (TOKENS, D), 1.0, 6.0, ((0, 32),))
    norm_gain = jnp.clip(1.0 + 0.1 * jax.random.normal(splits[2], (N_SEGMENT, D), jnp.float32), 0.5, 1.5)
    qkv_weight = noise(splits[3], (N_SEGMENT, 3, D, H * DH), D ** -0.5, 0.1875, ((0, 32), (3, 8)))
    out_weight = noise(splits[4], (N_SEGMENT, H * DH, D), (H * DH) ** -0.5, 0.1875, ((0, 32), (1, 8)))
    up_weight = noise(splits[5], (N_SEGMENT, D, FF), D ** -0.5, 0.1875, ((0, 32), (2, 8)))
    down_weight = noise(splits[6], (N_SEGMENT, FF, D), FF ** -0.5, 0.09375, ((0, 32), (1, 8)))
    logit_scale = jnp.clip(jnp.exp(math.log(16.0) - 1.3862944 * jax.random.uniform(splits[7], (N_SEGMENT, H), jnp.float32) ** block_levels(splits[7], (N_SEGMENT, H), ((0, 32), (1, 8)), -0.2, 0.2)), 4.0, 16.0)
    neighbour_table = draw_neighbour_table(jax.random.fold_in(splits[11], 71), 0)
    valid_table = draw_valid_table(jax.random.fold_in(splits[11], 71), 0)
    patch_of_segment = jax.random.permutation(splits[10], N_SEGMENT).astype(jnp.int32)
    return {"layer_input": layer_input, "cotangent": cotangent, "norm_gain": norm_gain, "qkv_weight": qkv_weight, "out_weight": out_weight, "up_weight": up_weight, "down_weight": down_weight, "logit_scale": logit_scale, "neighbour_table": neighbour_table, "valid_table": valid_table, "patch_of_segment": patch_of_segment}


root_half = 0.7071067811865476
normal_peak = 0.3989422804014327

def batched_product(form, left, right):
    return jnp.einsum(form, left.astype(jnp.float32), right.astype(jnp.float32))

def layer_terms(layer_rows, grad_rows, gain, qkv_part, out_part, up_part, down_part, scale, neighbours, valid_slots):
    tok_count = layer_rows.shape[0]
    head_count = scale.shape[0]
    col_count = out_part.shape[0]
    head_dim = col_count // head_count
    block_count = tok_count // BLK
    as_float = layer_rows.astype(jnp.float32)
    centred = as_float - lax.optimization_barrier(jnp.mean(as_float, -1, keepdims=True))
    inv_spread = lax.rsqrt(lax.optimization_barrier(jnp.mean(centred * centred, -1, keepdims=True)) + 1e-05)
    standard = centred * inv_spread
    unit_scaled = (standard * gain).astype(jnp.bfloat16)
    projected = [jnp.dot(unit_scaled, qkv_part[member], preferred_element_type=jnp.float32) for member in range(3)]
    raw_query = projected[0].reshape(tok_count, head_count, head_dim)
    raw_key = projected[1].reshape(tok_count, head_count, head_dim)
    inv_query = lax.rsqrt(lax.optimization_barrier(jnp.sum(raw_query * raw_query, -1, keepdims=True)) + 1e-06)
    inv_key = lax.rsqrt(lax.optimization_barrier(jnp.sum(raw_key * raw_key, -1, keepdims=True)) + 1e-06)
    q_unit = (raw_query * inv_query).astype(jnp.bfloat16).reshape(block_count, BLK, head_count, head_dim)
    k_unit = (raw_key * inv_key).astype(jnp.bfloat16).reshape(block_count, BLK, head_count, head_dim)
    values = projected[2].astype(jnp.bfloat16).reshape(block_count, BLK, head_count, head_dim)
    k_near = k_unit[neighbours]
    v_near = values[neighbours]
    cosine = batched_product('bihd,bjthd->bhijt', q_unit, k_near)
    scale_b = scale[None, :, None, None, None]
    live_slots = valid_slots.astype(jnp.float32)[:, None, None, :, None]
    exponent = jnp.exp(scale_b * cosine - scale_b) * live_slots
    weights = exponent / lax.optimization_barrier(jnp.sum(exponent, (3, 4), keepdims=True))
    weights_b = weights.astype(jnp.bfloat16)
    attended = batched_product('bhijt,bjthd->bihd', weights_b, v_near).astype(jnp.bfloat16).reshape(tok_count, col_count)
    pre_act = jnp.dot(unit_scaled, up_part, preferred_element_type=jnp.float32)
    normal_cdf = 0.5 * (1.0 + lax.erf(pre_act * root_half))
    activated = (pre_act * normal_cdf).astype(jnp.bfloat16)
    grad_down = jnp.dot(activated.T, grad_rows, preferred_element_type=jnp.float32).astype(jnp.bfloat16)
    d_act = jnp.dot(grad_rows, down_part.T, preferred_element_type=jnp.float32)
    slope = normal_cdf + pre_act * jnp.exp(-0.5 * pre_act * pre_act) * normal_peak
    d_pre = (d_act * slope).astype(jnp.bfloat16)
    grad_up = jnp.dot(unit_scaled.T, d_pre, preferred_element_type=jnp.float32).astype(jnp.bfloat16)
    d_normed = jnp.dot(d_pre, up_part.T, preferred_element_type=jnp.float32)
    d_att = jnp.dot(grad_rows, out_part.T, preferred_element_type=jnp.float32).astype(jnp.bfloat16)
    grad_out = jnp.dot(attended.T, grad_rows, preferred_element_type=jnp.float32).astype(jnp.bfloat16)
    d_att_blocks = d_att.reshape(block_count, BLK, head_count, head_dim)
    d_weights = batched_product('bihd,bjthd->bhijt', d_att_blocks, v_near)
    inner_sum = lax.optimization_barrier(jnp.sum(weights * d_weights, (3, 4), keepdims=True))
    d_score = weights * (d_weights - inner_sum)
    grad_scale = lax.optimization_barrier(jnp.sum(d_score * cosine, (0, 2, 3, 4)))
    d_cos = (d_score * scale_b).astype(jnp.bfloat16)
    d_q_unit = batched_product('bhijt,bjthd->bihd', d_cos, k_near).reshape(tok_count, head_count, head_dim)
    key_terms = batched_product('bhijt,bihd->bjthd', d_cos, q_unit)
    value_terms = batched_product('bhijt,bihd->bjthd', weights_b, d_att_blocks)
    one_hot = (neighbours[:, :, None] == jnp.arange(block_count, dtype=jnp.int32)[None, None, :]).astype(jnp.float32)
    d_k_unit = jnp.einsum('bjm,bjthd->mthd', one_hot, key_terms, precision=lax.Precision.HIGHEST).reshape(tok_count, head_count, head_dim)
    d_values = jnp.einsum('bjm,bjthd->mthd', one_hot, value_terms, precision=lax.Precision.HIGHEST).reshape(tok_count, col_count)
    d_raw_query = inv_query * d_q_unit - inv_query ** 3 * lax.optimization_barrier(jnp.sum(d_q_unit * raw_query, -1, keepdims=True)) * raw_query
    d_raw_key = inv_key * d_k_unit - inv_key ** 3 * lax.optimization_barrier(jnp.sum(d_k_unit * raw_key, -1, keepdims=True)) * raw_key
    d_raw = jnp.stack([d_raw_query.reshape(tok_count, col_count), d_raw_key.reshape(tok_count, col_count), d_values]).astype(jnp.bfloat16)
    grad_qkv = jnp.stack([jnp.dot(unit_scaled.T, d_raw[member], preferred_element_type=jnp.float32) for member in range(3)]).astype(jnp.bfloat16)
    for member in range(3):
        d_normed = d_normed + jnp.dot(d_raw[member], qkv_part[member].T, preferred_element_type=jnp.float32)
    return (d_normed, standard, inv_spread, grad_qkv, grad_out, grad_up, grad_down, grad_scale)

def norm_back(d_normed, grad_rows, standard, inv_spread, gain):
    scaled = d_normed * gain
    first_mean = lax.optimization_barrier(jnp.mean(scaled, -1, keepdims=True))
    second_mean = lax.optimization_barrier(jnp.mean(scaled * standard, -1, keepdims=True))
    d_input = (grad_rows.astype(jnp.float32) + inv_spread * (scaled - first_mean - standard * second_mean)).astype(jnp.bfloat16)
    gain_grad = lax.optimization_barrier(jnp.sum(d_normed * standard, 0))
    return (d_input, gain_grad)

def reference(layer_input, cotangent, norm_gain, qkv_weight, out_weight, up_weight, down_weight, logit_scale, neighbour_table, valid_table, patch_of_segment):
    col_count = H * DH // N_TP
    hidden_part = FF // N_TP
    segment_inputs = layer_input.reshape(N_SEGMENT, TOK, D)
    segment_grads = cotangent.reshape(N_SEGMENT, TOK, D)

    def one_segment(packed):
        layer_rows, grad_rows, gain, qkv_segment, out_segment, up_segment, down_segment, scale_segment, patch_id = packed
        neighbours = neighbour_table[patch_id]
        valid_slots = valid_table[patch_id]
        groups = (qkv_segment.reshape(3, D, N_TP, col_count).transpose(2, 0, 1, 3), out_segment.reshape(N_TP, col_count, D), up_segment.reshape(D, N_TP, hidden_part).transpose(1, 0, 2), down_segment.reshape(N_TP, hidden_part, D), scale_segment.reshape(N_TP, H // N_TP))

        def one_group(member):
            return layer_terms(layer_rows, grad_rows, gain, member[0], member[1], member[2], member[3], member[4], neighbours, valid_slots)
        d_normed, standard, inv_spread, grad_qkv, grad_out, grad_up, grad_down, grad_scale = lax.map(one_group, groups)
        rounded = lax.optimization_barrier(d_normed.astype(jnp.bfloat16)).astype(jnp.float32)
        total = lax.optimization_barrier(jnp.sum(rounded, 0))
        d_input, gain_grad = norm_back(total, grad_rows, standard[0], inv_spread[0], gain)
        return (d_input, grad_qkv.transpose(1, 2, 0, 3).reshape(3, D, H * DH), grad_out.reshape(H * DH, D), grad_up.transpose(1, 0, 2).reshape(D, FF), grad_down.reshape(FF, D), gain_grad, grad_scale.reshape(H))
    d_input, grad_qkv, grad_out, grad_up, grad_down, grad_gain, grad_scale = lax.map(one_segment, (segment_inputs, segment_grads, norm_gain, qkv_weight, out_weight, up_weight, down_weight, logit_scale, patch_of_segment))
    received = jnp.roll(d_input, -1, axis=0).reshape(N_SEGMENT * TOK, D)
    return (received, grad_qkv, grad_out, grad_up, grad_down, grad_gain, grad_scale)
```

```python
import functools

import jax
import jax.numpy as jnp
from jax import lax
from jax.experimental import pallas as pl
from jax.experimental.pallas import tpu as pltpu
from jax.sharding import PartitionSpec as P

BLK = 128
ROWS = 32

root_half = 0.7071067811865476
normal_peak = 0.3989422804014327

F32 = jnp.float32
BF16 = jnp.bfloat16


def dot_nn(left, right):
    return lax.dot_general(left, right, (((1,), (0,)), ((), ())), preferred_element_type=F32)


def dot_nt(left, right):
    return lax.dot_general(left, right, (((1,), (1,)), ((), ())), preferred_element_type=F32)


def dot_tn(left, right):
    return lax.dot_general(left, right, (((0,), (0,)), ((), ())), preferred_element_type=F32)


def section_kernel(
    patch_ref,
    near_ref,
    valid_ref,
    scale_ref,
    gain_ref,
    x_hbm,
    g_hbm,
    qkv_hbm,
    out_hbm,
    up_hbm,
    down_hbm,
    part_ref,
    grad_scale_ref,
    grad_qkv_hbm,
    grad_out_hbm,
    grad_up_hbm,
    grad_down_hbm,
    x_v,
    g_v,
    w_v,
    v_v,
    normed,
    raw,
    back,
    q_heads,
    k_all,
    v_all,
    datt_heads,
    cosine,
    d_weight,
    weight_b,
    d_cos,
    left_t,
    mask,
    hidden,
    d_all,
    grad_w,
    grad_v,
    in_sem,
    out_sem,
):
    tokens, width = x_v.shape
    cols = out_hbm.shape[0]
    units = down_hbm.shape[0]
    half = cols // 2
    blocks = tokens // BLK

    loads = [
        pltpu.make_async_copy(x_hbm, x_v, in_sem.at[0]),
        pltpu.make_async_copy(qkv_hbm.at[0, 0], w_v.at[:, pl.ds(0, cols)], in_sem.at[1]),
        pltpu.make_async_copy(qkv_hbm.at[0, 1], w_v.at[:, pl.ds(cols, cols)], in_sem.at[2]),
        pltpu.make_async_copy(qkv_hbm.at[0, 2], w_v.at[:, pl.ds(2 * cols, cols)], in_sem.at[3]),
        pltpu.make_async_copy(g_hbm, g_v, in_sem.at[4]),
        pltpu.make_async_copy(out_hbm, v_v.at[pl.ds(0, cols), :], in_sem.at[5]),
        pltpu.make_async_copy(up_hbm.at[0], w_v.at[:, pl.ds(3 * cols, units)], in_sem.at[6]),
        pltpu.make_async_copy(down_hbm, v_v.at[pl.ds(cols, units), :], in_sem.at[7]),
    ]
    for load in loads:
        load.start()

    patch = patch_ref[0]
    for b in range(blocks):
        for m in range(blocks):
            live = jnp.int32(0)
            for j in range(blocks):
                live = live + jnp.where(near_ref[patch, b, j] == m, valid_ref[patch, b, j], 0)
            mask[b, :, m * BLK : (m + 1) * BLK] = jnp.full((8, BLK), live, jnp.int32).astype(F32)

    loads[0].wait()

    def norm_rows(i, carry):
        at = pl.ds(pl.multiple_of(i * ROWS, ROWS), ROWS)
        value = x_v[at, :].astype(F32)
        centred = value - jnp.mean(value, -1, keepdims=True)
        inv_spread = lax.rsqrt(jnp.mean(centred * centred, -1, keepdims=True) + 1e-05)
        normed[at, :] = (centred * inv_spread * gain_ref[...]).astype(BF16)
        return carry

    lax.fori_loop(0, tokens // ROWS, norm_rows, 0, unroll=2)

    for load in loads[1:6]:
        load.wait()
    raw[:, : 3 * cols] = dot_nn(normed[...], w_v[:, : 3 * cols])
    loads[6].wait()
    raw[:, 3 * cols :] = dot_nn(normed[...], w_v[:, 3 * cols :])
    loads[7].wait()
    back[...] = dot_nt(g_v[...], v_v[...])

    def head_spread(total, first):
        low = lax.rsqrt(jnp.sum(jnp.where(first, total, 0.0), -1, keepdims=True) + 1e-06)
        high = lax.rsqrt(jnp.sum(jnp.where(first, 0.0, total), -1, keepdims=True) + 1e-06)
        return jnp.where(first, low, high)

    def head_sums(total, first):
        low = jnp.sum(jnp.where(first, total, 0.0), -1, keepdims=True)
        high = jnp.sum(jnp.where(first, 0.0, total), -1, keepdims=True)
        return jnp.where(first, low, high)

    for b in range(blocks):
        at = slice(b * BLK, (b + 1) * BLK)
        first = lax.broadcasted_iota(jnp.int32, (BLK, cols), 1) < half
        top = lax.broadcasted_iota(jnp.int32, (cols, BLK), 0) < half
        raw_q = raw[at, :cols]
        unit = raw_q * head_spread(raw_q * raw_q, first)
        d_att = back[at, :cols]
        for member, source, heads in ((0, unit, q_heads), (1, d_att, datt_heads)):
            heads[0, at, :] = jnp.where(first, source, 0.0).astype(BF16)
            heads[1, at, :] = jnp.where(first, 0.0, source).astype(BF16)
            flipped = source.T
            left_t[member, :, b * BLK : (b + 1) * BLK] = jnp.where(top, flipped, 0.0).astype(BF16)
            left_t[member, :, tokens + b * BLK : tokens + (b + 1) * BLK] = jnp.where(
                top, 0.0, flipped
            ).astype(BF16)
        raw_k = raw[at, cols : 2 * cols]
        k_all[at, :] = (raw_k * head_spread(raw_k * raw_k, first)).astype(BF16)
        v_all[at, :] = raw[at, 2 * cols : 3 * cols].astype(BF16)

    for h in range(2):
        cosine[h] = dot_nt(q_heads[h], k_all[...])
        d_weight[h] = dot_nt(datt_heads[h], v_all[...])

    def attend_rows(i, sums):
        at = pl.ds(pl.multiple_of(i * ROWS, ROWS), ROWS)
        live = mask[i // (BLK // ROWS), 0:1, :]
        fresh = []
        for h in range(2):
            factor = scale_ref[0, h]
            cos = cosine[h, at, :]
            exponent = jnp.exp(factor * cos - factor) * live
            weights = exponent * (1.0 / jnp.sum(exponent, -1, keepdims=True))
            d_w = d_weight[h, at, :]
            inner = jnp.sum(weights * d_w, -1, keepdims=True)
            d_score = weights * (d_w - inner)
            spot = pl.ds(pl.multiple_of(h * tokens + i * ROWS, ROWS), ROWS)
            weight_b[spot, :] = weights.astype(BF16)
            d_cos[spot, :] = (d_score * factor).astype(BF16)
            fresh.append(sums[h] + d_score * cos)
        return tuple(fresh)

    def hidden_rows(i):
        at = pl.ds(pl.multiple_of(i * ROWS, ROWS), ROWS)
        pre = raw[at, 3 * cols :]
        cdf = 0.5 * (1.0 + lax.erf(pre * root_half))
        hidden[at, cols:] = (pre * cdf).astype(BF16)
        slope = cdf + pre * jnp.exp(-0.5 * pre * pre) * normal_peak
        d_all[at, 3 * cols :] = (back[at, cols:] * slope).astype(BF16)

    def both_rows(i, sums):
        hidden_rows(i)
        return attend_rows(i, sums)

    zero = jnp.zeros((ROWS, tokens), F32)
    sums = lax.fori_loop(0, tokens // ROWS, both_rows, (zero, zero))
    for h in range(2):
        grad_scale_ref[0, h] = jnp.sum(sums[h])

    first = lax.broadcasted_iota(jnp.int32, (tokens, cols), 1) < half
    hidden[:, :cols] = jnp.where(
        first, dot_nn(weight_b[:tokens, :], v_all[...]), dot_nn(weight_b[tokens:, :], v_all[...])
    ).astype(BF16)
    d_q = jnp.where(
        first, dot_nn(d_cos[:tokens, :], k_all[...]), dot_nn(d_cos[tokens:, :], k_all[...])
    )
    d_k = dot_nn(left_t[0], d_cos[...]).T
    d_all[:, 2 * cols : 3 * cols] = dot_nn(left_t[1], weight_b[...]).T.astype(BF16)
    for i, d_unit in ((0, d_q), (1, d_k)):
        value = raw[:, i * cols : (i + 1) * cols]
        inv = head_spread(value * value, first)
        inner = head_sums(d_unit * value, first)
        d_all[:, i * cols : (i + 1) * cols] = (
            inv * d_unit - inv * inv * inv * inner * value
        ).astype(BF16)

    part_ref[...] = dot_nt(d_all[...], w_v[...]).astype(BF16)

    stores = []
    step = 256
    for start in range(0, width, step):
        at = slice(start, start + step)
        grad_w[at, :] = dot_tn(normed[:, at], d_all[...]).astype(BF16)
    for i in range(3):
        stores.append(
            pltpu.make_async_copy(
                grad_w.at[:, pl.ds(i * cols, cols)], grad_qkv_hbm.at[0, i], out_sem.at[i]
            )
        )
    stores.append(
        pltpu.make_async_copy(grad_w.at[:, pl.ds(3 * cols, units)], grad_up_hbm.at[0], out_sem.at[3])
    )
    for store in stores:
        store.start()
    grad_v[...] = dot_tn(hidden[...], g_v[...]).astype(BF16)
    stores.append(
        pltpu.make_async_copy(grad_v.at[pl.ds(0, cols), :], grad_out_hbm, out_sem.at[4])
    )
    stores.append(
        pltpu.make_async_copy(grad_v.at[pl.ds(cols, units), :], grad_down_hbm, out_sem.at[5])
    )
    for store in stores[4:]:
        store.start()
    for store in stores:
        store.wait()


def section_terms(x, g, gain, qkv, out, up, down, scale, near, valid, patch):
    tokens, width = x.shape
    cols = out.shape[1]
    units = down.shape[1]
    wide = 3 * cols + units
    tall = cols + units
    smem = pl.BlockSpec(memory_space=pltpu.SMEM)
    vmem = pl.BlockSpec(memory_space=pltpu.VMEM)
    hbm = pl.BlockSpec(memory_space=pl.ANY)
    shape = jax.ShapeDtypeStruct
    return pl.pallas_call(
        section_kernel,
        out_shape=(
            shape((tokens, width), BF16),
            shape((1, 2), F32),
            shape(qkv.shape, BF16),
            shape((cols, width), BF16),
            shape(up.shape, BF16),
            shape((units, width), BF16),
        ),
        in_specs=[smem, smem, smem, smem, vmem, hbm, hbm, hbm, hbm, hbm, hbm],
        out_specs=[vmem, smem, hbm, hbm, hbm, hbm],
        scratch_shapes=[
            pltpu.VMEM((tokens, width), BF16),
            pltpu.VMEM((tokens, width), BF16),
            pltpu.VMEM((width, wide), BF16),
            pltpu.VMEM((tall, width), BF16),
            pltpu.VMEM((tokens, width), BF16),
            pltpu.VMEM((tokens, wide), F32),
            pltpu.VMEM((tokens, tall), F32),
            pltpu.VMEM((2, tokens, cols), BF16),
            pltpu.VMEM((tokens, cols), BF16),
            pltpu.VMEM((tokens, cols), BF16),
            pltpu.VMEM((2, tokens, cols), BF16),
            pltpu.VMEM((2, tokens, tokens), F32),
            pltpu.VMEM((2, tokens, tokens), F32),
            pltpu.VMEM((2 * tokens, tokens), BF16),
            pltpu.VMEM((2 * tokens, tokens), BF16),
            pltpu.VMEM((2, cols, 2 * tokens), BF16),
            pltpu.VMEM((tokens // BLK, 8, tokens), F32),
            pltpu.VMEM((tokens, tall), BF16),
            pltpu.VMEM((tokens, wide), BF16),
            pltpu.VMEM((width, wide), BF16),
            pltpu.VMEM((tall, width), BF16),
            pltpu.SemaphoreType.DMA((8,)),
            pltpu.SemaphoreType.DMA((6,)),
        ],
        compiler_params=pltpu.CompilerParams(vmem_limit_bytes=56 * 1024 * 1024),
        name="section_terms",
    )(patch, near, valid, scale, gain, x, g, qkv, out[0], up, down[0])


def in_blocks(value, dim, devices):
    lengths = value.shape
    pieces = value.reshape(*lengths[:dim], devices, lengths[dim] // devices, *lengths[dim + 1 :])
    return jnp.moveaxis(pieces, dim, 0)


def summed_on_arrival(value, axis, dim):
    devices = lax.axis_size(axis)
    pieces = lax.all_to_all(in_blocks(value, dim, devices), axis, 0, 0, tiled=True)
    return jnp.sum(pieces.astype(jnp.float32), axis=0)


def from_everyone(value, axis):
    copies = jnp.broadcast_to(value, (lax.axis_size(axis), *value.shape))
    return lax.all_to_all(copies, axis, split_axis=0, concat_axis=0, tiled=True)


def taken_together(value, axis):
    return from_everyone(value, axis).sum(axis=0)


def from_behind(value, axis, by):
    devices = lax.axis_size(axis)
    return lax.ppermute(value, axis, [(i, (i + by) % devices) for i in range(devices)])


def joined_along(pieces, dim):
    lengths = list(pieces.shape[1:])
    lengths[dim] *= pieces.shape[0]
    return jnp.moveaxis(pieces, 0, dim).reshape(lengths)


def gathered_copies(value, axis, dim):
    return joined_along(from_everyone(value, axis), dim)


def norm_back(d_normed, grad_rows, standard, inv_spread, gain):
    scaled = d_normed * gain
    first_mean = jnp.mean(scaled, -1, keepdims=True)
    second_mean = jnp.mean(scaled * standard, -1, keepdims=True)
    d_input = (
        grad_rows.astype(jnp.float32) + inv_spread * (scaled - first_mean - standard * second_mean)
    ).astype(jnp.bfloat16)
    gain_grad = jnp.sum(d_normed * standard, 0)
    return (d_input, gain_grad)


def shards(x, g, gain, qkv, out, up, down, scale, near, valid, patch):
    part, grad_scale, grad_qkv, grad_out, grad_up, grad_down = section_terms(
        x, g, gain, qkv, out, up, down, scale, near, valid, patch
    )
    row_count = x.shape[0] // lax.axis_size("tp")
    row_start = lax.axis_index("tp") * row_count
    share = summed_on_arrival(part, "tp", 0)
    grad_share = lax.dynamic_slice_in_dim(g, row_start, row_count, 0)
    as_float = lax.dynamic_slice_in_dim(x, row_start, row_count, 0).astype(jnp.float32)
    centred = as_float - jnp.mean(as_float, -1, keepdims=True)
    inv_spread = lax.rsqrt(jnp.mean(centred * centred, -1, keepdims=True) + 1e-05)
    input_share, gain_part = norm_back(share, grad_share, centred * inv_spread, inv_spread, gain[0])
    gain_grad = taken_together(gain_part, "tp")
    shifted = from_behind(input_share, "segment", -1)
    received = gathered_copies(shifted, "tp", 0)
    return (
        received,
        grad_qkv,
        grad_out[None],
        grad_up,
        grad_down[None],
        gain_grad[None],
        grad_scale,
    )


def solution(mesh):
    placed = (
        P("segment", None),
        P("segment", None),
        P("segment", None),
        P("segment", None, None, "tp"),
        P("segment", "tp", None),
        P("segment", None, "tp"),
        P("segment", "tp", None),
        P("segment", "tp"),
        P(),
        P(),
        P("segment"),
    )
    return jax.shard_map(
        shards,
        mesh=mesh,
        in_specs=placed,
        out_specs=(
            P("segment", None),
            P("segment", None, None, "tp"),
            P("segment", "tp", None),
            P("segment", None, "tp"),
            P("segment", "tp", None),
            P("segment", None),
            P("segment", "tp"),
        ),
        check_vma=False,
    )
```

```python
import functools

import jax
import jax.numpy as jnp
from jax import lax
from jax.experimental import pallas as pl
from jax.experimental.pallas import tpu as pltpu
from jax.sharding import PartitionSpec as P

BLK = 128
ROWS = 32

root_half = 0.7071067811865476
normal_peak = 0.3989422804014327

F32 = jnp.float32
BF16 = jnp.bfloat16


def dot_nn(left, right):
    return lax.dot_general(left, right, (((1,), (0,)), ((), ())), preferred_element_type=F32)


def dot_nt(left, right):
    return lax.dot_general(left, right, (((1,), (1,)), ((), ())), preferred_element_type=F32)


def dot_tn(left, right):
    return lax.dot_general(left, right, (((0,), (0,)), ((), ())), preferred_element_type=F32)


def section_kernel(
    patch_ref,
    near_ref,
    valid_ref,
    scale_ref,
    gain_ref,
    x_hbm,
    g_hbm,
    qkv_hbm,
    out_hbm,
    up_hbm,
    down_hbm,
    part_ref,
    grad_scale_ref,
    grad_qkv_hbm,
    grad_out_hbm,
    grad_up_hbm,
    grad_down_hbm,
    x_v,
    g_v,
    w_v,
    v_v,
    normed,
    raw,
    back,
    q_heads,
    k_all,
    v_all,
    datt_heads,
    cosine,
    d_weight,
    weight_b,
    d_cos,
    left_t,
    mask,
    hidden,
    d_all,
    grad_w,
    grad_v,
    in_sem,
    out_sem,
):
    tokens, width = x_v.shape
    cols = out_hbm.shape[0]
    units = down_hbm.shape[0]
    half = cols // 2
    blocks = tokens // BLK

    loads = [
        pltpu.make_async_copy(x_hbm, x_v, in_sem.at[0]),
        pltpu.make_async_copy(qkv_hbm.at[0, 0], w_v.at[:, pl.ds(0, cols)], in_sem.at[1]),
        pltpu.make_async_copy(qkv_hbm.at[0, 1], w_v.at[:, pl.ds(cols, cols)], in_sem.at[2]),
        pltpu.make_async_copy(qkv_hbm.at[0, 2], w_v.at[:, pl.ds(2 * cols, cols)], in_sem.at[3]),
        pltpu.make_async_copy(g_hbm, g_v, in_sem.at[4]),
        pltpu.make_async_copy(out_hbm, v_v.at[pl.ds(0, cols), :], in_sem.at[5]),
        pltpu.make_async_copy(up_hbm.at[0], w_v.at[:, pl.ds(3 * cols, units)], in_sem.at[6]),
        pltpu.make_async_copy(down_hbm, v_v.at[pl.ds(cols, units), :], in_sem.at[7]),
    ]
    for load in loads:
        load.start()

    patch = patch_ref[0]
    for b in range(blocks):
        for m in range(blocks):
            live = jnp.int32(0)
            for j in range(blocks):
                live = live + jnp.where(near_ref[patch, b, j] == m, valid_ref[patch, b, j], 0)
            mask[b, :, m * BLK : (m + 1) * BLK] = jnp.full((8, BLK), live, jnp.int32).astype(F32)

    loads[0].wait()

    def norm_rows(i, carry):
        at = pl.ds(pl.multiple_of(i * ROWS, ROWS), ROWS)
        value = x_v[at, :].astype(F32)
        centred = value - jnp.mean(value, -1, keepdims=True)
        inv_spread = lax.rsqrt(jnp.mean(centred * centred, -1, keepdims=True) + 1e-05)
        normed[at, :] = (centred * inv_spread * gain_ref[...]).astype(BF16)
        return carry

    lax.fori_loop(0, tokens // ROWS, norm_rows, 0, unroll=2)

    for load in loads[1:6]:
        load.wait()
    raw[:, : 3 * cols] = dot_nn(normed[...], w_v[:, : 3 * cols])
    loads[6].wait()
    raw[:, 3 * cols :] = dot_nn(normed[...], w_v[:, 3 * cols :])
    loads[7].wait()
    back[...] = dot_nt(g_v[...], v_v[...])

    def head_spread(total, first):
        low = lax.rsqrt(jnp.sum(jnp.where(first, total, 0.0), -1, keepdims=True) + 1e-06)
        high = lax.rsqrt(jnp.sum(jnp.where(first, 0.0, total), -1, keepdims=True) + 1e-06)
        return jnp.where(first, low, high)

    def head_sums(total, first):
        low = jnp.sum(jnp.where(first, total, 0.0), -1, keepdims=True)
        high = jnp.sum(jnp.where(first, 0.0, total), -1, keepdims=True)
        return jnp.where(first, low, high)

    for b in range(blocks):
        at = slice(b * BLK, (b + 1) * BLK)
        first = lax.broadcasted_iota(jnp.int32, (BLK, cols), 1) < half
        top = lax.broadcasted_iota(jnp.int32, (cols, BLK), 0) < half
        raw_q = raw[at, :cols]
        unit = raw_q * head_spread(raw_q * raw_q, first)
        d_att = back[at, :cols]
        for member, source, heads in ((0, unit, q_heads), (1, d_att, datt_heads)):
            heads[0, at, :] = jnp.where(first, source, 0.0).astype(BF16)
            heads[1, at, :] = jnp.where(first, 0.0, source).astype(BF16)
            flipped = source.T
            left_t[member, :, b * BLK : (b + 1) * BLK] = jnp.where(top, flipped, 0.0).astype(BF16)
            left_t[member, :, tokens + b * BLK : tokens + (b + 1) * BLK] = jnp.where(
                top, 0.0, flipped
            ).astype(BF16)
        raw_k = raw[at, cols : 2 * cols]
        k_all[at, :] = (raw_k * head_spread(raw_k * raw_k, first)).astype(BF16)
        v_all[at, :] = raw[at, 2 * cols : 3 * cols].astype(BF16)

    for h in range(2):
        cosine[h] = dot_nt(q_heads[h], k_all[...])
        d_weight[h] = dot_nt(datt_heads[h], v_all[...])

    def attend_rows(i, sums):
        at = pl.ds(pl.multiple_of(i * ROWS, ROWS), ROWS)
        live = mask[i // (BLK // ROWS), 0:1, :]
        fresh = []
        for h in range(2):
            factor = scale_ref[0, h]
            cos = cosine[h, at, :]
            exponent = jnp.exp(factor * cos - factor) * live
            weights = exponent * (1.0 / jnp.sum(exponent, -1, keepdims=True))
            d_w = d_weight[h, at, :]
            inner = jnp.sum(weights * d_w, -1, keepdims=True)
            d_score = weights * (d_w - inner)
            spot = pl.ds(pl.multiple_of(h * tokens + i * ROWS, ROWS), ROWS)
            weight_b[spot, :] = weights.astype(BF16)
            d_cos[spot, :] = (d_score * factor).astype(BF16)
            fresh.append(sums[h] + d_score * cos)
        return tuple(fresh)

    def hidden_rows(i):
        at = pl.ds(pl.multiple_of(i * ROWS, ROWS), ROWS)
        pre = raw[at, 3 * cols :]
        cdf = 0.5 * (1.0 + lax.erf(pre * root_half))
        hidden[at, cols:] = (pre * cdf).astype(BF16)
        slope = cdf + pre * jnp.exp(-0.5 * pre * pre) * normal_peak
        d_all[at, 3 * cols :] = (back[at, cols:] * slope).astype(BF16)

    def both_rows(i, sums):
        hidden_rows(i)
        return attend_rows(i, sums)

    zero = jnp.zeros((ROWS, tokens), F32)
    sums = lax.fori_loop(0, tokens // ROWS, both_rows, (zero, zero))
    for h in range(2):
        grad_scale_ref[0, h] = jnp.sum(sums[h])

    first = lax.broadcasted_iota(jnp.int32, (tokens, cols), 1) < half
    hidden[:, :cols] = jnp.where(
        first, dot_nn(weight_b[:tokens, :], v_all[...]), dot_nn(weight_b[tokens:, :], v_all[...])
    ).astype(BF16)
    d_q = jnp.where(
        first, dot_nn(d_cos[:tokens, :], k_all[...]), dot_nn(d_cos[tokens:, :], k_all[...])
    )
    d_k = dot_nn(left_t[0], d_cos[...]).T
    d_all[:, 2 * cols : 3 * cols] = dot_nn(left_t[1], weight_b[...]).T.astype(BF16)
    for i, d_unit in ((0, d_q), (1, d_k)):
        value = raw[:, i * cols : (i + 1) * cols]
        inv = head_spread(value * value, first)
        inner = head_sums(d_unit * value, first)
        d_all[:, i * cols : (i + 1) * cols] = (
            inv * d_unit - inv * inv * inv * inner * value
        ).astype(BF16)

    part_ref[...] = dot_nt(d_all[...], w_v[...]).astype(BF16)

    stores = []
    step = 256
    for start in range(0, width, step):
        at = slice(start, start + step)
        grad_w[at, :] = dot_tn(normed[:, at], d_all[...]).astype(BF16)
    for i in range(3):
        stores.append(
            pltpu.make_async_copy(
                grad_w.at[:, pl.ds(i * cols, cols)], grad_qkv_hbm.at[0, i], out_sem.at[i]
            )
        )
    stores.append(
        pltpu.make_async_copy(grad_w.at[:, pl.ds(3 * cols, units)], grad_up_hbm.at[0], out_sem.at[3])
    )
    for store in stores:
        store.start()
    grad_v[...] = dot_tn(hidden[...], g_v[...]).astype(BF16)
    stores.append(
        pltpu.make_async_copy(grad_v.at[pl.ds(0, cols), :], grad_out_hbm, out_sem.at[4])
    )
    stores.append(
        pltpu.make_async_copy(grad_v.at[pl.ds(cols, units), :], grad_down_hbm, out_sem.at[5])
    )
    for store in stores[4:]:
        store.start()
    for store in stores:
        store.wait()


def section_terms(x, g, gain, qkv, out, up, down, scale, near, valid, patch):
    tokens, width = x.shape
    cols = out.shape[1]
    units = down.shape[1]
    wide = 3 * cols + units
    tall = cols + units
    smem = pl.BlockSpec(memory_space=pltpu.SMEM)
    vmem = pl.BlockSpec(memory_space=pltpu.VMEM)
    hbm = pl.BlockSpec(memory_space=pl.ANY)
    shape = jax.ShapeDtypeStruct
    return pl.pallas_call(
        section_kernel,
        out_shape=(
            shape((tokens, width), BF16),
            shape((1, 2), F32),
            shape(qkv.shape, BF16),
            shape((cols, width), BF16),
            shape(up.shape, BF16),
            shape((units, width), BF16),
        ),
        in_specs=[smem, smem, smem, smem, vmem, hbm, hbm, hbm, hbm, hbm, hbm],
        out_specs=[vmem, smem, hbm, hbm, hbm, hbm],
        scratch_shapes=[
            pltpu.VMEM((tokens, width), BF16),
            pltpu.VMEM((tokens, width), BF16),
            pltpu.VMEM((width, wide), BF16),
            pltpu.VMEM((tall, width), BF16),
            pltpu.VMEM((tokens, width), BF16),
            pltpu.VMEM((tokens, wide), F32),
            pltpu.VMEM((tokens, tall), F32),
            pltpu.VMEM((2, tokens, cols), BF16),
            pltpu.VMEM((tokens, cols), BF16),
            pltpu.VMEM((tokens, cols), BF16),
            pltpu.VMEM((2, tokens, cols), BF16),
            pltpu.VMEM((2, tokens, tokens), F32),
            pltpu.VMEM((2, tokens, tokens), F32),
            pltpu.VMEM((2 * tokens, tokens), BF16),
            pltpu.VMEM((2 * tokens, tokens), BF16),
            pltpu.VMEM((2, cols, 2 * tokens), BF16),
            pltpu.VMEM((tokens // BLK, 8, tokens), F32),
            pltpu.VMEM((tokens, tall), BF16),
            pltpu.VMEM((tokens, wide), BF16),
            pltpu.VMEM((width, wide), BF16),
            pltpu.VMEM((tall, width), BF16),
            pltpu.SemaphoreType.DMA((8,)),
            pltpu.SemaphoreType.DMA((6,)),
        ],
        compiler_params=pltpu.CompilerParams(vmem_limit_bytes=56 * 1024 * 1024),
        name="section_terms",
    )(patch, near, valid, scale, gain, x, g, qkv, out[0], up, down[0])


CHUNK = 16
LAG = 2
MESH = pl.DeviceIdType.MESH


def relay_kernel(
    sections,
    members,
    part,
    gain_ref,
    x_hbm,
    g_hbm,
    received,
    gain_out,
    pair_buf,
    line_buf,
    line_out,
    d_input,
    x_q,
    g_q,
    standard,
    spread,
    landed,
    gain_sum,
    gain_buf,
    load_sem,
    pair_send,
    pair_recv,
    line_send,
    line_recv,
    shift_send,
    ring_send,
    ring_recv,
    fan_send,
    fan_recv,
    gain_send,
    gain_recv,
    out_sem,
):
    tokens, width = part.shape
    quarter = tokens // 4
    chunks = quarter // CHUNK
    last = members // 2 - 1
    segment = lax.axis_index("segment")
    member = lax.axis_index("tp")
    chip = member // 2
    core = member % 2
    partner = chip * 2 + (1 - core)
    target = (segment + sections - 1) % sections
    source = (segment + 1) % sections
    half = sections // 2
    turn_out = jnp.where(target // half == segment // half, 0, 1)
    turn_in = jnp.where(source // half == segment // half, 0, 1)
    target_chip = jnp.where(turn_out == 1, last - chip, chip)
    source_chip = jnp.where(turn_in == 1, last - chip, chip)
    at_target = (target, target_chip * 2 + core)
    at_source = (source, source_chip * 2 + core)

    barrier = pltpu.get_barrier_semaphore()
    for other in range(1, members):
        pl.semaphore_signal(
            barrier, 1, device_id=(segment, (member + other) % members), device_id_type=MESH
        )
    pl.semaphore_signal(barrier, 1, device_id=at_target, device_id_type=MESH)
    pl.semaphore_signal(barrier, 1, device_id=at_source, device_id_type=MESH)

    is_end = jnp.logical_or(chip == 0, chip == last)
    owned = core * 2 + jnp.where(chip == last, 1, 0)
    mine = pl.ds(pl.multiple_of(owned * quarter, quarter), quarter)
    x_load = pltpu.make_async_copy(x_hbm.at[mine, :], x_q, load_sem.at[0])
    g_load = pltpu.make_async_copy(g_hbm.at[mine, :], g_q, load_sem.at[1])

    @pl.when(is_end)
    def _():
        x_load.start()
        g_load.start()

    pl.semaphore_wait(barrier, members + 1)

    def rows_of(block, piece):
        return pl.ds(pl.multiple_of(block * quarter + piece * CHUNK, CHUNK), CHUNK)

    def piece_of(piece):
        return pl.ds(pl.multiple_of(piece * CHUNK, CHUNK), CHUNK)

    def pair_copy(way, piece):
        return pltpu.make_async_remote_copy(
            src_ref=part.at[rows_of((1 - core) * 2 + way, piece), :],
            dst_ref=pair_buf.at[way, piece_of(piece), :],
            send_sem=pair_send.at[way, piece],
            recv_sem=pair_recv.at[way, piece],
            device_id=(segment, partner),
            device_id_type=MESH,
        )

    def place(way):
        return chip if way == 1 else last - chip

    def beyond(way):
        ahead = jnp.minimum(chip + 1, last) if way == 1 else jnp.maximum(chip - 1, 0)
        return (segment, ahead * 2 + core)

    def line_copy(way, piece):
        return pltpu.make_async_remote_copy(
            src_ref=line_out.at[way, piece_of(piece), :],
            dst_ref=line_buf.at[way, piece_of(piece), :],
            send_sem=line_send.at[way, piece],
            recv_sem=line_recv.at[way, piece],
            device_id=beyond(way),
            device_id_type=MESH,
        )

    def shift_copy(way, piece):
        entry = jnp.where(turn_out == 1, way, 1 - way)
        return pltpu.make_async_remote_copy(
            src_ref=d_input.at[piece_of(piece), :],
            dst_ref=landed.at[rows_of(core * 2 + way, piece), :],
            send_sem=shift_send.at[piece],
            recv_sem=ring_recv.at[entry, piece],
            device_id=at_target,
            device_id_type=MESH,
        )

    def ring_block(way):
        return jnp.where(turn_in == 1, way, 1 - way)

    def ring_copy(way, piece):
        rows = landed.at[rows_of(core * 2 + ring_block(way), piece), :]
        return pltpu.make_async_remote_copy(
            src_ref=rows,
            dst_ref=rows,
            send_sem=ring_send.at[way, piece],
            recv_sem=ring_recv.at[way, piece],
            device_id=beyond(way),
            device_id_type=MESH,
        )

    def fan_copy(way, piece):
        rows = landed.at[rows_of(core * 2 + ring_block(way), piece), :]
        return pltpu.make_async_remote_copy(
            src_ref=rows,
            dst_ref=rows,
            send_sem=fan_send.at[way, piece],
            recv_sem=fan_recv.at[way, piece],
            device_id=(segment, partner),
            device_id_type=MESH,
        )

    def fan_arrival(way, piece):
        rows = landed.at[rows_of((1 - core) * 2 + ring_block(way), piece), :]
        return pltpu.make_async_remote_copy(
            src_ref=rows,
            dst_ref=rows,
            send_sem=fan_send.at[way, piece],
            recv_sem=fan_recv.at[way, piece],
            device_id=(segment, partner),
            device_id_type=MESH,
        )

    def out_copy(side, way, piece):
        owner = core if side == 0 else 1 - core
        rows = rows_of(owner * 2 + ring_block(way), piece)
        return pltpu.make_async_copy(
            landed.at[rows, :], received.at[rows, :], out_sem.at[side, way, piece]
        )

    def gain_copy(slot, other):
        return pltpu.make_async_remote_copy(
            src_ref=gain_sum,
            dst_ref=gain_buf.at[slot],
            send_sem=gain_send.at[other - 1],
            recv_sem=gain_recv.at[slot],
            device_id=(segment, (member + other) % members),
            device_id_type=MESH,
        )

    def start_pairs(piece, carry):
        for way in range(2):
            pair_copy(way, piece).start()
        return carry

    lax.fori_loop(0, chunks, start_pairs, 0)

    @pl.when(is_end)
    def _():
        x_load.wait()
        g_load.wait()
        gain_sum[...] = jnp.zeros_like(gain_sum)

        def norm_rows(i, carry):
            at = piece_of(i)
            value = x_q[at, :].astype(F32)
            centred = value - jnp.mean(value, -1, keepdims=True)
            inv = lax.rsqrt(jnp.mean(centred * centred, -1, keepdims=True) + 1e-05)
            standard[at, :] = centred * inv
            spread[at, :] = jnp.broadcast_to(inv, (CHUNK, 128))
            return carry

        lax.fori_loop(0, chunks, norm_rows, 0)

    def reduce_step(way, piece):
        spot = place(way)
        at = piece_of(piece)
        pair_copy(way, piece).wait_recv()
        total = (
            part[rows_of(core * 2 + way, piece), :].astype(F32)
            + pair_buf[way, at, :].astype(F32)
        )

        @pl.when(spot == 0)
        def _():
            line_out[way, at, :] = total.astype(BF16)
            line_copy(way, piece).start()

        @pl.when(jnp.logical_and(spot > 0, spot < last))
        def _():
            line_copy(way, piece).wait_recv()
            line_out[way, at, :] = (total + line_buf[way, at, :].astype(F32)).astype(BF16)
            line_copy(way, piece).start()

        @pl.when(spot == last)
        def _():
            line_copy(way, piece).wait_recv()
            d_normed = total + line_buf[way, at, :].astype(F32)
            unit = standard[at, :]
            scaled = d_normed * gain_ref[...]
            first_mean = jnp.mean(scaled, -1, keepdims=True)
            second_mean = jnp.mean(scaled * unit, -1, keepdims=True)
            inv = spread[at, :][:, :1]
            d_input[at, :] = (
                g_q[at, :].astype(F32) + inv * (scaled - first_mean - unit * second_mean)
            ).astype(BF16)
            shift_copy(way, piece).start()
            gain_sum[...] += jnp.sum(d_normed * unit, 0, keepdims=True)

            @pl.when(piece == chunks - 1)
            def _():
                slot = jnp.where(chip == last, 2, 0) + core
                for other in range(1, members):
                    gain_copy(slot, other).start()

    def gather_step(way, piece):
        ring_copy(way, piece).wait_recv()

        @pl.when(place(way) < last)
        def _():
            ring_copy(way, piece).start()

        fan_copy(way, piece).start()
        out_copy(0, way, piece).start()

    steps = chunks + LAG * (2 * last + 1)

    def slot(k, carry):
        for way in range(2):
            piece = k - LAG * place(way)

            @pl.when(jnp.logical_and(piece >= 0, piece < chunks))
            def _():
                reduce_step(way, piece)

        for way in range(2):
            piece = k - LAG * (last + 1 + place(way))

            @pl.when(jnp.logical_and(piece >= 0, piece < chunks))
            def _():
                gather_step(way, piece)

        return carry

    lax.fori_loop(0, steps, slot, 0)

    def finish(piece, carry):
        for way in range(2):
            fan_arrival(way, piece).wait_recv()
            out_copy(1, way, piece).start()
        return carry

    lax.fori_loop(0, chunks, finish, 0)

    owners = (0, 1, members - 2, members - 1)
    total = jnp.zeros_like(gain_sum[...])
    for slot_index, owner in enumerate(owners):

        @pl.when(member != owner)
        def _():
            gain_copy(slot_index, 1).wait_recv()

        @pl.when(member == owner)
        def _():
            gain_buf[slot_index] = gain_sum[...]

        total = total + gain_buf[slot_index]
    gain_out[...] = total

    def settle(piece, carry):
        for way in range(2):
            pair_copy(way, piece).wait_send()
            fan_copy(way, piece).wait_send()
            out_copy(0, way, piece).wait()
            out_copy(1, way, piece).wait()

            @pl.when(place(way) < last)
            def _():
                line_copy(way, piece).wait_send()
                ring_copy(way, piece).wait_send()

            @pl.when(place(way) == last)
            def _():
                shift_copy(way, piece).wait_send()

        return carry

    lax.fori_loop(0, chunks, settle, 0)

    @pl.when(is_end)
    def _():
        for other in range(1, members):
            gain_copy(0, other).wait_send()


def relayed(sections, members, part, x, g, gain):
    tokens, width = x.shape
    quarter = tokens // 4
    chunks = quarter // CHUNK
    vmem = pl.BlockSpec(memory_space=pltpu.VMEM)
    hbm = pl.BlockSpec(memory_space=pl.ANY)
    dma = pltpu.SemaphoreType.DMA
    return pl.pallas_call(
        functools.partial(relay_kernel, sections, members),
        out_shape=(
            jax.ShapeDtypeStruct((tokens, width), BF16),
            jax.ShapeDtypeStruct((1, width), F32),
        ),
        in_specs=[vmem, vmem, hbm, hbm],
        out_specs=[hbm, vmem],
        scratch_shapes=[
            pltpu.VMEM((2, quarter, width), BF16),
            pltpu.VMEM((2, quarter, width), BF16),
            pltpu.VMEM((2, quarter, width), BF16),
            pltpu.VMEM((quarter, width), BF16),
            pltpu.VMEM((quarter, width), BF16),
            pltpu.VMEM((quarter, width), BF16),
            pltpu.VMEM((quarter, width), F32),
            pltpu.VMEM((quarter, 128), F32),
            pltpu.VMEM((tokens, width), BF16),
            pltpu.VMEM((1, width), F32),
            pltpu.VMEM((4, 1, width), F32),
            dma((2,)),
            dma((2, chunks)),
            dma((2, chunks)),
            dma((2, chunks)),
            dma((2, chunks)),
            dma((chunks,)),
            dma((2, chunks)),
            dma((2, chunks)),
            dma((2, chunks)),
            dma((2, chunks)),
            dma((members - 1,)),
            dma((4,)),
            dma((2, 2, chunks)),
        ],
        compiler_params=pltpu.CompilerParams(
            collective_id=0, has_side_effects=True, vmem_limit_bytes=32 * 1024 * 1024
        ),
        name="relayed",
    )(part, gain, x, g)


def shards(sections, members, x, g, gain, qkv, out, up, down, scale, near, valid, patch):
    part, grad_scale, grad_qkv, grad_out, grad_up, grad_down = section_terms(
        x, g, gain, qkv, out, up, down, scale, near, valid, patch
    )
    received, gain_grad = relayed(sections, members, part, x, g, gain)
    return (
        received,
        grad_qkv,
        grad_out[None],
        grad_up,
        grad_down[None],
        gain_grad,
        grad_scale,
    )


def solution(mesh):
    placed = (
        P("segment", None),
        P("segment", None),
        P("segment", None),
        P("segment", None, None, "tp"),
        P("segment", "tp", None),
        P("segment", None, "tp"),
        P("segment", "tp", None),
        P("segment", "tp"),
        P(),
        P(),
        P("segment"),
    )
    return jax.shard_map(
        functools.partial(shards, mesh.shape["segment"], mesh.shape["tp"]),
        mesh=mesh,
        in_specs=placed,
        out_specs=(
            P("segment", None),
            P("segment", None, None, "tp"),
            P("segment", "tp", None),
            P("segment", None, "tp"),
            P("segment", "tp", None),
            P("segment", None),
            P("segment", "tp"),
        ),
        check_vma=False,
    )
```

```python
import functools

import jax
import jax.numpy as jnp
from jax import lax
from jax.experimental import pallas as pl
from jax.experimental.pallas import tpu as pltpu
from jax.sharding import PartitionSpec as P

BLK = 128
ROWS = 32

root_half = 0.7071067811865476
normal_peak = 0.3989422804014327

F32 = jnp.float32
BF16 = jnp.bfloat16


def dot_nn(left, right):
    return lax.dot_general(left, right, (((1,), (0,)), ((), ())), preferred_element_type=F32)


def dot_nt(left, right):
    return lax.dot_general(left, right, (((1,), (1,)), ((), ())), preferred_element_type=F32)


def dot_tn(left, right):
    return lax.dot_general(left, right, (((0,), (0,)), ((), ())), preferred_element_type=F32)


CHUNK = 16
LAG = 4
GRAD_AT_END = 8
GRAD_AT_MIDDLE = 0
MESH = pl.DeviceIdType.MESH


def section_kernel(
    sections,
    members,
    patch_ref,
    near_ref,
    valid_ref,
    scale_ref,
    gain_ref,
    x_hbm,
    g_hbm,
    qkv_hbm,
    out_hbm,
    up_hbm,
    down_hbm,
    received,
    gain_out,
    grad_scale_ref,
    grad_qkv,
    grad_out,
    grad_up,
    grad_down,
    x_v,
    g_v,
    w_v,
    v_v,
    normed,
    raw,
    back,
    q_heads,
    k_all,
    v_all,
    datt_heads,
    cosine,
    d_weight,
    weight_b,
    d_cos,
    left_t,
    mask,
    hidden,
    d_all,
    part,
    pair_buf,
    line_buf,
    line_out,
    d_input,
    standard,
    spread,
    landed,
    gain_sum,
    gain_buf,
    in_sem,
    pair_send,
    pair_recv,
    line_send,
    line_recv,
    shift_send,
    ring_send,
    ring_recv,
    fan_send,
    fan_recv,
    gain_send,
    gain_recv,
    out_sem,
):
    tokens, width = x_v.shape
    cols = out_hbm.shape[0]
    units = down_hbm.shape[0]
    head = cols // 2
    blocks = tokens // BLK

    quarter = tokens // 4
    chunks = quarter // CHUNK
    last = members // 2 - 1
    segment = lax.axis_index("segment")
    member = lax.axis_index("tp")
    chip = member // 2
    core = member % 2
    partner = chip * 2 + (1 - core)
    target = (segment + sections - 1) % sections
    source = (segment + 1) % sections
    half = sections // 2
    turn_out = jnp.where(target // half == segment // half, 0, 1)
    turn_in = jnp.where(source // half == segment // half, 0, 1)
    target_chip = jnp.where(turn_out == 1, last - chip, chip)
    source_chip = jnp.where(turn_in == 1, last - chip, chip)
    at_target = (target, target_chip * 2 + core)
    at_source = (source, source_chip * 2 + core)

    barrier = pltpu.get_barrier_semaphore()
    for other in range(1, members):
        pl.semaphore_signal(
            barrier, 1, device_id=(segment, (member + other) % members), device_id_type=MESH
        )
    pl.semaphore_signal(barrier, 1, device_id=at_target, device_id_type=MESH)
    pl.semaphore_signal(barrier, 1, device_id=at_source, device_id_type=MESH)

    loads = [
        pltpu.make_async_copy(x_hbm, x_v, in_sem.at[0]),
        pltpu.make_async_copy(qkv_hbm.at[0, 0], w_v.at[:, pl.ds(0, cols)], in_sem.at[1]),
        pltpu.make_async_copy(qkv_hbm.at[0, 1], w_v.at[:, pl.ds(cols, cols)], in_sem.at[2]),
        pltpu.make_async_copy(qkv_hbm.at[0, 2], w_v.at[:, pl.ds(2 * cols, cols)], in_sem.at[3]),
        pltpu.make_async_copy(g_hbm, g_v, in_sem.at[4]),
        pltpu.make_async_copy(out_hbm, v_v.at[pl.ds(0, cols), :], in_sem.at[5]),
        pltpu.make_async_copy(up_hbm.at[0], w_v.at[:, pl.ds(3 * cols, units)], in_sem.at[6]),
        pltpu.make_async_copy(down_hbm, v_v.at[pl.ds(cols, units), :], in_sem.at[7]),
    ]
    for load in loads:
        load.start()

    patch = patch_ref[0]
    for b in range(blocks):
        for m in range(blocks):
            live = jnp.int32(0)
            for j in range(blocks):
                live = live + jnp.where(near_ref[b, j, patch] == m, valid_ref[b, j, patch], 0)
            mask[b, :, m * BLK : (m + 1) * BLK] = jnp.full((8, BLK), live, jnp.int32).astype(F32)

    loads[0].wait()

    def norm_rows(i, carry):
        at = pl.ds(pl.multiple_of(i * ROWS, ROWS), ROWS)
        value = x_v[at, :].astype(F32)
        centred = value - jnp.mean(value, -1, keepdims=True)
        inv_spread = lax.rsqrt(jnp.mean(centred * centred, -1, keepdims=True) + 1e-05)
        normed[at, :] = (centred * inv_spread * gain_ref[...]).astype(BF16)
        return carry

    lax.fori_loop(0, tokens // ROWS, norm_rows, 0, unroll=2)

    for load in loads[1:6]:
        load.wait()
    raw[:, : 3 * cols] = dot_nn(normed[...], w_v[:, : 3 * cols])
    loads[6].wait()
    raw[:, 3 * cols :] = dot_nn(normed[...], w_v[:, 3 * cols :])
    loads[7].wait()
    back[...] = dot_nt(g_v[...], v_v[...])

    def head_spread(total, first):
        low = lax.rsqrt(jnp.sum(jnp.where(first, total, 0.0), -1, keepdims=True) + 1e-06)
        high = lax.rsqrt(jnp.sum(jnp.where(first, 0.0, total), -1, keepdims=True) + 1e-06)
        return jnp.where(first, low, high)

    def head_sums(total, first):
        low = jnp.sum(jnp.where(first, total, 0.0), -1, keepdims=True)
        high = jnp.sum(jnp.where(first, 0.0, total), -1, keepdims=True)
        return jnp.where(first, low, high)

    for b in range(blocks):
        at = slice(b * BLK, (b + 1) * BLK)
        first = lax.broadcasted_iota(jnp.int32, (BLK, cols), 1) < head
        top = lax.broadcasted_iota(jnp.int32, (cols, BLK), 0) < head
        raw_q = raw[at, :cols]
        unit = raw_q * head_spread(raw_q * raw_q, first)
        d_att = back[at, :cols]
        for turn, spread_in, heads in ((0, unit, q_heads), (1, d_att, datt_heads)):
            heads[0, at, :] = jnp.where(first, spread_in, 0.0).astype(BF16)
            heads[1, at, :] = jnp.where(first, 0.0, spread_in).astype(BF16)
            flipped = spread_in.T
            left_t[turn, :, b * BLK : (b + 1) * BLK] = jnp.where(top, flipped, 0.0).astype(BF16)
            left_t[turn, :, tokens + b * BLK : tokens + (b + 1) * BLK] = jnp.where(
                top, 0.0, flipped
            ).astype(BF16)
        raw_k = raw[at, cols : 2 * cols]
        k_all[at, :] = (raw_k * head_spread(raw_k * raw_k, first)).astype(BF16)
        v_all[at, :] = raw[at, 2 * cols : 3 * cols].astype(BF16)

    for h in range(2):
        cosine[h] = dot_nt(q_heads[h], k_all[...])
        d_weight[h] = dot_nt(datt_heads[h], v_all[...])

    def attend_rows(i, sums):
        at = pl.ds(pl.multiple_of(i * ROWS, ROWS), ROWS)
        live = mask[i // (BLK // ROWS), 0:1, :]
        fresh = []
        for h in range(2):
            factor = scale_ref[0, h]
            cos = cosine[h, at, :]
            exponent = jnp.exp(factor * cos - factor) * live
            weights = exponent * (1.0 / jnp.sum(exponent, -1, keepdims=True))
            d_w = d_weight[h, at, :]
            inner = jnp.sum(weights * d_w, -1, keepdims=True)
            d_score = weights * (d_w - inner)
            spot = pl.ds(pl.multiple_of(h * tokens + i * ROWS, ROWS), ROWS)
            weight_b[spot, :] = weights.astype(BF16)
            d_cos[spot, :] = (d_score * factor).astype(BF16)
            fresh.append(sums[h] + d_score * cos)
        return tuple(fresh)

    def hidden_rows(i):
        at = pl.ds(pl.multiple_of(i * ROWS, ROWS), ROWS)
        pre = raw[at, 3 * cols :]
        cdf = 0.5 * (1.0 + lax.erf(pre * root_half))
        hidden[at, cols:] = (pre * cdf).astype(BF16)
        slope = cdf + pre * jnp.exp(-0.5 * pre * pre) * normal_peak
        d_all[at, 3 * cols :] = (back[at, cols:] * slope).astype(BF16)

    def both_rows(i, sums):
        hidden_rows(i)
        return attend_rows(i, sums)

    zero = jnp.zeros((ROWS, tokens), F32)
    sums = lax.fori_loop(0, tokens // ROWS, both_rows, (zero, zero))
    for h in range(2):
        grad_scale_ref[0, h] = jnp.sum(sums[h])

    first = lax.broadcasted_iota(jnp.int32, (tokens, cols), 1) < head
    hidden[:, :cols] = jnp.where(
        first, dot_nn(weight_b[:tokens, :], v_all[...]), dot_nn(weight_b[tokens:, :], v_all[...])
    ).astype(BF16)
    d_q = jnp.where(
        first, dot_nn(d_cos[:tokens, :], k_all[...]), dot_nn(d_cos[tokens:, :], k_all[...])
    )
    d_k = dot_nn(left_t[0], d_cos[...]).T
    d_all[:, 2 * cols : 3 * cols] = dot_nn(left_t[1], weight_b[...]).T.astype(BF16)
    for i, d_unit in ((0, d_q), (1, d_k)):
        value = raw[:, i * cols : (i + 1) * cols]
        inv = head_spread(value * value, first)
        inner = head_sums(d_unit * value, first)
        d_all[:, i * cols : (i + 1) * cols] = (
            inv * d_unit - inv * inv * inv * inner * value
        ).astype(BF16)

    is_end = jnp.logical_or(chip == 0, chip == last)
    owned = core * 2 + jnp.where(chip == last, 1, 0)

    def rows_of(block, piece):
        return pl.ds(pl.multiple_of(block * quarter + piece * CHUNK, CHUNK), CHUNK)

    def piece_of(piece):
        return pl.ds(pl.multiple_of(piece * CHUNK, CHUNK), CHUNK)

    def pair_copy(way, piece):
        return pltpu.make_async_remote_copy(
            src_ref=part.at[rows_of((1 - core) * 2 + way, piece), :],
            dst_ref=pair_buf.at[way, piece_of(piece), :],
            send_sem=pair_send.at[way, piece],
            recv_sem=pair_recv.at[way, piece],
            device_id=(segment, partner),
            device_id_type=MESH,
        )

    def place(way):
        return chip if way == 1 else last - chip

    def beyond(way):
        ahead = jnp.minimum(chip + 1, last) if way == 1 else jnp.maximum(chip - 1, 0)
        return (segment, ahead * 2 + core)

    def line_copy(way, piece):
        return pltpu.make_async_remote_copy(
            src_ref=line_out.at[way, piece_of(piece), :],
            dst_ref=line_buf.at[way, piece_of(piece), :],
            send_sem=line_send.at[way, piece],
            recv_sem=line_recv.at[way, piece],
            device_id=beyond(way),
            device_id_type=MESH,
        )

    def shift_copy(way, piece):
        entry = jnp.where(turn_out == 1, way, 1 - way)
        return pltpu.make_async_remote_copy(
            src_ref=d_input.at[piece_of(piece), :],
            dst_ref=landed.at[rows_of(core * 2 + way, piece), :],
            send_sem=shift_send.at[piece],
            recv_sem=ring_recv.at[entry, piece],
            device_id=at_target,
            device_id_type=MESH,
        )

    def ring_block(way):
        return jnp.where(turn_in == 1, way, 1 - way)

    def ring_copy(way, piece):
        rows = landed.at[rows_of(core * 2 + ring_block(way), piece), :]
        return pltpu.make_async_remote_copy(
            src_ref=rows,
            dst_ref=rows,
            send_sem=ring_send.at[way, piece],
            recv_sem=ring_recv.at[way, piece],
            device_id=beyond(way),
            device_id_type=MESH,
        )

    def fan_copy(way, piece):
        rows = landed.at[rows_of(core * 2 + ring_block(way), piece), :]
        return pltpu.make_async_remote_copy(
            src_ref=rows,
            dst_ref=rows,
            send_sem=fan_send.at[way, piece],
            recv_sem=fan_recv.at[way, piece],
            device_id=(segment, partner),
            device_id_type=MESH,
        )

    def fan_arrival(way, piece):
        rows = landed.at[rows_of((1 - core) * 2 + ring_block(way), piece), :]
        return pltpu.make_async_remote_copy(
            src_ref=rows,
            dst_ref=rows,
            send_sem=fan_send.at[way, piece],
            recv_sem=fan_recv.at[way, piece],
            device_id=(segment, partner),
            device_id_type=MESH,
        )

    def out_copy(side, way, piece):
        owner = core if side == 0 else 1 - core
        rows = rows_of(owner * 2 + ring_block(way), piece)
        return pltpu.make_async_copy(
            landed.at[rows, :], received.at[rows, :], out_sem.at[side, way, piece]
        )

    def gain_copy(slot, other):
        return pltpu.make_async_remote_copy(
            src_ref=gain_sum,
            dst_ref=gain_buf.at[slot],
            send_sem=gain_send.at[other - 1],
            recv_sem=gain_recv.at[slot],
            device_id=(segment, (member + other) % members),
            device_id_type=MESH,
        )

    def start_pairs(piece, carry):
        for way in range(2):
            pair_copy(way, piece).start()
        return carry

    side = 2 * quarter
    theirs = pl.ds(pl.multiple_of((1 - core) * side, side), side)
    ours = pl.ds(pl.multiple_of(core * side, side), side)
    part[theirs, :] = dot_nt(d_all[theirs, :], w_v[...]).astype(BF16)
    pl.semaphore_wait(barrier, members + 1)
    lax.fori_loop(0, chunks, start_pairs, 0)
    part[ours, :] = dot_nt(d_all[ours, :], w_v[...]).astype(BF16)

    @pl.when(is_end)
    def _():
        gain_sum[...] = jnp.zeros_like(gain_sum)

        def norm_rows(i, carry):
            at = piece_of(i)
            value = x_v[rows_of(owned, i), :].astype(F32)
            centred = value - jnp.mean(value, -1, keepdims=True)
            inv = lax.rsqrt(jnp.mean(centred * centred, -1, keepdims=True) + 1e-05)
            standard[at, :] = centred * inv
            spread[at, :] = jnp.broadcast_to(inv, (CHUNK, 128))
            return carry

        lax.fori_loop(0, chunks, norm_rows, 0)

    def reduce_step(way, piece):
        spot = place(way)
        at = piece_of(piece)
        pair_copy(way, piece).wait_recv()
        total = (
            part[rows_of(core * 2 + way, piece), :].astype(F32)
            + pair_buf[way, at, :].astype(F32)
        )

        @pl.when(spot == 0)
        def _():
            line_out[way, at, :] = total.astype(BF16)
            line_copy(way, piece).start()

        @pl.when(jnp.logical_and(spot > 0, spot < last))
        def _():
            line_copy(way, piece).wait_recv()
            line_out[way, at, :] = (total + line_buf[way, at, :].astype(F32)).astype(BF16)
            line_copy(way, piece).start()

        @pl.when(spot == last)
        def _():
            line_copy(way, piece).wait_recv()
            d_normed = total + line_buf[way, at, :].astype(F32)
            unit = standard[at, :]
            scaled = d_normed * gain_ref[...]
            first_mean = jnp.mean(scaled, -1, keepdims=True)
            second_mean = jnp.mean(scaled * unit, -1, keepdims=True)
            inv = spread[at, :][:, :1]
            d_input[at, :] = (
                g_v[rows_of(owned, piece), :].astype(F32) + inv * (scaled - first_mean - unit * second_mean)
            ).astype(BF16)
            shift_copy(way, piece).start()
            gain_sum[...] += jnp.sum(d_normed * unit, 0, keepdims=True)

            @pl.when(piece == chunks - 1)
            def _():
                slot = jnp.where(chip == last, 2, 0) + core
                for other in range(1, members):
                    gain_copy(slot, other).start()

    def gather_step(way, piece):
        ring_copy(way, piece).wait_recv()

        @pl.when(place(way) < last)
        def _():
            ring_copy(way, piece).start()

        fan_copy(way, piece).start()
        out_copy(0, way, piece).start()

    steps = chunks + LAG * (2 * last + 1)

    wide_pieces = width // BLK
    tall_pieces = (cols + units) // BLK
    grad_start = jnp.where(is_end, GRAD_AT_END, GRAD_AT_MIDDLE)

    def grad_step(piece):
        @pl.when(jnp.logical_and(piece >= 0, piece < wide_pieces))
        def _():
            at = pl.ds(pl.multiple_of(piece * BLK, BLK), BLK)
            value = dot_tn(normed[:, at], d_all[...]).astype(BF16)
            for i in range(3):
                grad_qkv[0, i, at, :] = value[:, i * cols : (i + 1) * cols]
            grad_up[0, at, :] = value[:, 3 * cols :]

        @pl.when(piece == wide_pieces)
        def _():
            grad_out[...] = dot_tn(hidden[:, :cols], g_v[...]).astype(BF16)

        @pl.when(jnp.logical_and(piece > wide_pieces, piece < wide_pieces + tall_pieces))
        def _():
            spot = piece - wide_pieces
            at = pl.ds(pl.multiple_of(spot * BLK, BLK), BLK)
            down_at = pl.ds(pl.multiple_of(spot * BLK - cols, BLK), BLK)
            grad_down[down_at, :] = dot_tn(hidden[:, at], g_v[...]).astype(BF16)

    def slot(k, carry):
        for way in range(2):
            piece = k - LAG * place(way)

            @pl.when(jnp.logical_and(piece >= 0, piece < chunks))
            def _():
                reduce_step(way, piece)

        for way in range(2):
            piece = k - LAG * (last + 1 + place(way))

            @pl.when(jnp.logical_and(piece >= 0, piece < chunks))
            def _():
                gather_step(way, piece)

        grad_step(k - grad_start)
        return carry

    lax.fori_loop(0, steps, slot, 0)

    def finish(piece, carry):
        for way in range(2):
            fan_arrival(way, piece).wait_recv()
            out_copy(1, way, piece).start()
        return carry

    lax.fori_loop(0, chunks, finish, 0)

    owners = (0, 1, members - 2, members - 1)
    total = jnp.zeros_like(gain_sum[...])
    for slot_index, owner in enumerate(owners):

        @pl.when(member != owner)
        def _():
            gain_copy(slot_index, 1).wait_recv()

        @pl.when(member == owner)
        def _():
            gain_buf[slot_index] = gain_sum[...]

        total = total + gain_buf[slot_index]
    gain_out[...] = total

    def settle(piece, carry):
        for way in range(2):
            pair_copy(way, piece).wait_send()
            fan_copy(way, piece).wait_send()
            out_copy(0, way, piece).wait()
            out_copy(1, way, piece).wait()

            @pl.when(place(way) < last)
            def _():
                line_copy(way, piece).wait_send()
                ring_copy(way, piece).wait_send()

            @pl.when(place(way) == last)
            def _():
                shift_copy(way, piece).wait_send()

        return carry

    lax.fori_loop(0, chunks, settle, 0)

    @pl.when(is_end)
    def _():
        for other in range(1, members):
            gain_copy(0, other).wait_send()


def section(sections, members, x, g, gain, qkv, out, up, down, scale, near, valid, patch):
    tokens, width = x.shape
    cols = out.shape[1]
    units = down.shape[1]
    wide = 3 * cols + units
    tall = cols + units
    quarter = tokens // 4
    chunks = quarter // CHUNK
    smem = pl.BlockSpec(memory_space=pltpu.SMEM)
    vmem = pl.BlockSpec(memory_space=pltpu.VMEM)
    hbm = pl.BlockSpec(memory_space=pl.ANY)
    shape = jax.ShapeDtypeStruct
    dma = pltpu.SemaphoreType.DMA
    return pl.pallas_call(
        functools.partial(section_kernel, sections, members),
        out_shape=(
            shape((tokens, width), BF16),
            shape((1, width), F32),
            shape((1, 2), F32),
            shape(qkv.shape, BF16),
            shape((cols, width), BF16),
            shape(up.shape, BF16),
            shape((units, width), BF16),
        ),
        in_specs=[smem, smem, smem, smem, vmem, hbm, hbm, hbm, hbm, hbm, hbm],
        out_specs=[hbm, vmem, smem, vmem, vmem, vmem, vmem],
        scratch_shapes=[
            pltpu.VMEM((tokens, width), BF16),
            pltpu.VMEM((tokens, width), BF16),
            pltpu.VMEM((width, wide), BF16),
            pltpu.VMEM((tall, width), BF16),
            pltpu.VMEM((tokens, width), BF16),
            pltpu.VMEM((tokens, wide), F32),
            pltpu.VMEM((tokens, tall), F32),
            pltpu.VMEM((2, tokens, cols), BF16),
            pltpu.VMEM((tokens, cols), BF16),
            pltpu.VMEM((tokens, cols), BF16),
            pltpu.VMEM((2, tokens, cols), BF16),
            pltpu.VMEM((2, tokens, tokens), F32),
            pltpu.VMEM((2, tokens, tokens), F32),
            pltpu.VMEM((2 * tokens, tokens), BF16),
            pltpu.VMEM((2 * tokens, tokens), BF16),
            pltpu.VMEM((2, cols, 2 * tokens), BF16),
            pltpu.VMEM((tokens // BLK, 8, tokens), F32),
            pltpu.VMEM((tokens, tall), BF16),
            pltpu.VMEM((tokens, wide), BF16),
            pltpu.VMEM((tokens, width), BF16),
            pltpu.VMEM((2, quarter, width), BF16),
            pltpu.VMEM((2, quarter, width), BF16),
            pltpu.VMEM((2, quarter, width), BF16),
            pltpu.VMEM((quarter, width), BF16),
            pltpu.VMEM((quarter, width), F32),
            pltpu.VMEM((quarter, 128), F32),
            pltpu.VMEM((tokens, width), BF16),
            pltpu.VMEM((1, width), F32),
            pltpu.VMEM((4, 1, width), F32),
            dma((8,)),
            dma((2, chunks)),
            dma((2, chunks)),
            dma((2, chunks)),
            dma((2, chunks)),
            dma((chunks,)),
            dma((2, chunks)),
            dma((2, chunks)),
            dma((2, chunks)),
            dma((2, chunks)),
            dma((members - 1,)),
            dma((4,)),
            dma((2, 2, chunks)),
        ],
        compiler_params=pltpu.CompilerParams(
            collective_id=0, has_side_effects=True, vmem_limit_bytes=48 * 1024 * 1024
        ),
        name="section",
    )(
        patch,
        near.transpose(1, 2, 0),
        valid.transpose(1, 2, 0),
        scale,
        gain,
        x,
        g,
        qkv,
        out[0],
        up,
        down[0],
    )


def shards(sections, members, *arrays):
    received, gain_grad, grad_scale, grad_qkv, grad_out, grad_up, grad_down = section(
        sections, members, *arrays
    )
    return (
        received,
        grad_qkv,
        grad_out[None],
        grad_up,
        grad_down[None],
        gain_grad,
        grad_scale,
    )


def solution(mesh):
    placed = (
        P("segment", None),
        P("segment", None),
        P("segment", None),
        P("segment", None, None, "tp"),
        P("segment", "tp", None),
        P("segment", None, "tp"),
        P("segment", "tp", None),
        P("segment", "tp"),
        P(),
        P(),
        P("segment"),
    )
    return jax.shard_map(
        functools.partial(shards, mesh.shape["segment"], mesh.shape["tp"]),
        mesh=mesh,
        in_specs=placed,
        out_specs=(
            P("segment", None),
            P("segment", None, None, "tp"),
            P("segment", "tp", None),
            P("segment", None, "tp"),
            P("segment", "tp", None),
            P("segment", None),
            P("segment", "tp"),
        ),
        check_vma=False,
    )
```

```python
import functools

import jax
import jax.numpy as jnp
from jax import lax
from jax.experimental import pallas as pl
from jax.experimental.pallas import tpu as pltpu
from jax.sharding import PartitionSpec as P

BLK = 128
ROWS = 32

root_half = 0.7071067811865476
normal_peak = 0.3989422804014327

F32 = jnp.float32
BF16 = jnp.bfloat16


def dot_nn(left, right):
    return lax.dot_general(left, right, (((1,), (0,)), ((), ())), preferred_element_type=F32)


def dot_nt(left, right):
    return lax.dot_general(left, right, (((1,), (1,)), ((), ())), preferred_element_type=F32)


def dot_tn(left, right):
    return lax.dot_general(left, right, (((0,), (0,)), ((), ())), preferred_element_type=F32)


CHUNK = 16
LAG = 4
GRAD_AT_END = 8
GRAD_AT_MIDDLE = 0
MESH = pl.DeviceIdType.MESH


def section_kernel(
    sections,
    members,
    patch_hbm,
    near_hbm,
    valid_hbm,
    scale_hbm,
    gain_hbm,
    x_hbm,
    g_hbm,
    qkv_hbm,
    out_hbm,
    up_hbm,
    down_hbm,
    received,
    gain_out,
    grad_scale_ref,
    grad_qkv,
    grad_out,
    grad_up,
    grad_down,
    x_v,
    g_v,
    w_v,
    v_v,
    normed,
    raw,
    back,
    q_heads,
    k_all,
    v_all,
    datt_heads,
    cosine,
    d_weight,
    weight_b,
    d_cos,
    left_t,
    mask,
    hidden,
    d_all,
    part,
    pair_buf,
    line_buf,
    line_out,
    d_input,
    standard,
    spread,
    landed,
    gain_sum,
    gain_buf,
    patch_ref,
    near_ref,
    valid_ref,
    scale_ref,
    gain_ref,
    in_sem,
    pair_send,
    pair_recv,
    line_send,
    line_recv,
    shift_send,
    ring_send,
    ring_recv,
    fan_send,
    fan_recv,
    gain_send,
    gain_recv,
    out_sem,
):
    tokens, width = x_v.shape
    cols = out_hbm.shape[0]
    units = down_hbm.shape[0]
    head = cols // 2
    blocks = tokens // BLK

    quarter = tokens // 4
    chunks = quarter // CHUNK
    last = members // 2 - 1
    segment = lax.axis_index("segment")
    member = lax.axis_index("tp")
    chip = member // 2
    core = member % 2
    partner = chip * 2 + (1 - core)
    target = (segment + sections - 1) % sections
    source = (segment + 1) % sections
    half = sections // 2
    turn_out = jnp.where(target // half == segment // half, 0, 1)
    turn_in = jnp.where(source // half == segment // half, 0, 1)
    target_chip = jnp.where(turn_out == 1, last - chip, chip)
    source_chip = jnp.where(turn_in == 1, last - chip, chip)
    at_target = (target, target_chip * 2 + core)
    at_source = (source, source_chip * 2 + core)

    barrier = pltpu.get_barrier_semaphore()
    for other in range(1, members):
        pl.semaphore_signal(
            barrier, 1, device_id=(segment, (member + other) % members), device_id_type=MESH
        )
    pl.semaphore_signal(barrier, 1, device_id=at_target, device_id_type=MESH)
    pl.semaphore_signal(barrier, 1, device_id=at_source, device_id_type=MESH)

    loads = [
        pltpu.make_async_copy(x_hbm, x_v, in_sem.at[0]),
        pltpu.make_async_copy(qkv_hbm.at[0, 0], w_v.at[:, pl.ds(0, cols)], in_sem.at[1]),
        pltpu.make_async_copy(qkv_hbm.at[0, 1], w_v.at[:, pl.ds(cols, cols)], in_sem.at[2]),
        pltpu.make_async_copy(qkv_hbm.at[0, 2], w_v.at[:, pl.ds(2 * cols, cols)], in_sem.at[3]),
        pltpu.make_async_copy(g_hbm, g_v, in_sem.at[4]),
        pltpu.make_async_copy(out_hbm, v_v.at[pl.ds(0, cols), :], in_sem.at[5]),
        pltpu.make_async_copy(up_hbm.at[0], w_v.at[:, pl.ds(3 * cols, units)], in_sem.at[6]),
        pltpu.make_async_copy(down_hbm, v_v.at[pl.ds(cols, units), :], in_sem.at[7]),
    ]
    small = [
        pltpu.make_async_copy(patch_hbm, patch_ref, in_sem.at[8]),
        pltpu.make_async_copy(near_hbm, near_ref, in_sem.at[9]),
        pltpu.make_async_copy(valid_hbm, valid_ref, in_sem.at[10]),
        pltpu.make_async_copy(scale_hbm, scale_ref, in_sem.at[11]),
        pltpu.make_async_copy(gain_hbm, gain_ref, in_sem.at[12]),
    ]
    for load in loads[:1] + small + loads[1:]:
        load.start()
    for load in small:
        load.wait()

    patch = patch_ref[0]
    for b in range(blocks):
        for m in range(blocks):
            live = jnp.int32(0)
            for j in range(blocks):
                live = live + jnp.where(near_ref[b, j, patch] == m, valid_ref[b, j, patch], 0)
            mask[b, :, m * BLK : (m + 1) * BLK] = jnp.full((8, BLK), live, jnp.int32).astype(F32)

    loads[0].wait()

    def norm_rows(i, carry):
        at = pl.ds(pl.multiple_of(i * ROWS, ROWS), ROWS)
        value = x_v[at, :].astype(F32)
        centred = value - jnp.mean(value, -1, keepdims=True)
        inv_spread = lax.rsqrt(jnp.mean(centred * centred, -1, keepdims=True) + 1e-05)
        normed[at, :] = (centred * inv_spread * gain_ref[...]).astype(BF16)
        return carry

    lax.fori_loop(0, tokens // ROWS, norm_rows, 0, unroll=2)

    for load in loads[1:6]:
        load.wait()
    raw[:, : 3 * cols] = dot_nn(normed[...], w_v[:, : 3 * cols])
    loads[6].wait()
    raw[:, 3 * cols :] = dot_nn(normed[...], w_v[:, 3 * cols :])
    loads[7].wait()
    back[...] = dot_nt(g_v[...], v_v[...])

    def head_spread(total, first):
        low = lax.rsqrt(jnp.sum(jnp.where(first, total, 0.0), -1, keepdims=True) + 1e-06)
        high = lax.rsqrt(jnp.sum(jnp.where(first, 0.0, total), -1, keepdims=True) + 1e-06)
        return jnp.where(first, low, high)

    def head_sums(total, first):
        low = jnp.sum(jnp.where(first, total, 0.0), -1, keepdims=True)
        high = jnp.sum(jnp.where(first, 0.0, total), -1, keepdims=True)
        return jnp.where(first, low, high)

    for b in range(blocks):
        at = slice(b * BLK, (b + 1) * BLK)
        first = lax.broadcasted_iota(jnp.int32, (BLK, cols), 1) < head
        top = lax.broadcasted_iota(jnp.int32, (cols, BLK), 0) < head
        raw_q = raw[at, :cols]
        unit = raw_q * head_spread(raw_q * raw_q, first)
        d_att = back[at, :cols]
        for turn, spread_in, heads in ((0, unit, q_heads), (1, d_att, datt_heads)):
            heads[0, at, :] = jnp.where(first, spread_in, 0.0).astype(BF16)
            heads[1, at, :] = jnp.where(first, 0.0, spread_in).astype(BF16)
            flipped = spread_in.T
            left_t[turn, :, b * BLK : (b + 1) * BLK] = jnp.where(top, flipped, 0.0).astype(BF16)
            left_t[turn, :, tokens + b * BLK : tokens + (b + 1) * BLK] = jnp.where(
                top, 0.0, flipped
            ).astype(BF16)
        raw_k = raw[at, cols : 2 * cols]
        k_all[at, :] = (raw_k * head_spread(raw_k * raw_k, first)).astype(BF16)
        v_all[at, :] = raw[at, 2 * cols : 3 * cols].astype(BF16)

    for h in range(2):
        cosine[h] = dot_nt(q_heads[h], k_all[...])
        d_weight[h] = dot_nt(datt_heads[h], v_all[...])

    def attend_rows(i, sums):
        at = pl.ds(pl.multiple_of(i * ROWS, ROWS), ROWS)
        live = mask[i // (BLK // ROWS), 0:1, :]
        fresh = []
        for h in range(2):
            factor = scale_ref[0, h]
            cos = cosine[h, at, :]
            exponent = jnp.exp(factor * cos - factor) * live
            weights = exponent * (1.0 / jnp.sum(exponent, -1, keepdims=True))
            d_w = d_weight[h, at, :]
            inner = jnp.sum(weights * d_w, -1, keepdims=True)
            d_score = weights * (d_w - inner)
            spot = pl.ds(pl.multiple_of(h * tokens + i * ROWS, ROWS), ROWS)
            weight_b[spot, :] = weights.astype(BF16)
            d_cos[spot, :] = (d_score * factor).astype(BF16)
            fresh.append(sums[h] + d_score * cos)
        return tuple(fresh)

    def hidden_rows(i):
        at = pl.ds(pl.multiple_of(i * ROWS, ROWS), ROWS)
        pre = raw[at, 3 * cols :]
        cdf = 0.5 * (1.0 + lax.erf(pre * root_half))
        hidden[at, cols:] = (pre * cdf).astype(BF16)
        slope = cdf + pre * jnp.exp(-0.5 * pre * pre) * normal_peak
        d_all[at, 3 * cols :] = (back[at, cols:] * slope).astype(BF16)

    def both_rows(i, sums):
        hidden_rows(i)
        return attend_rows(i, sums)

    zero = jnp.zeros((ROWS, tokens), F32)
    sums = lax.fori_loop(0, tokens // ROWS, both_rows, (zero, zero))
    grad_scale_ref[...] = jnp.where(
        lax.broadcasted_iota(jnp.int32, (1, 2), 1) == 0, jnp.sum(sums[0]), jnp.sum(sums[1])
    )

    first = lax.broadcasted_iota(jnp.int32, (tokens, cols), 1) < head
    hidden[:, :cols] = jnp.where(
        first, dot_nn(weight_b[:tokens, :], v_all[...]), dot_nn(weight_b[tokens:, :], v_all[...])
    ).astype(BF16)
    d_q = jnp.where(
        first, dot_nn(d_cos[:tokens, :], k_all[...]), dot_nn(d_cos[tokens:, :], k_all[...])
    )
    d_k = dot_nn(left_t[0], d_cos[...]).T
    d_all[:, 2 * cols : 3 * cols] = dot_nn(left_t[1], weight_b[...]).T.astype(BF16)
    for i, d_unit in ((0, d_q), (1, d_k)):
        value = raw[:, i * cols : (i + 1) * cols]
        inv = head_spread(value * value, first)
        inner = head_sums(d_unit * value, first)
        d_all[:, i * cols : (i + 1) * cols] = (
            inv * d_unit - inv * inv * inv * inner * value
        ).astype(BF16)

    is_end = jnp.logical_or(chip == 0, chip == last)
    owned = core * 2 + jnp.where(chip == last, 1, 0)

    def rows_of(block, piece):
        return pl.ds(pl.multiple_of(block * quarter + piece * CHUNK, CHUNK), CHUNK)

    def piece_of(piece):
        return pl.ds(pl.multiple_of(piece * CHUNK, CHUNK), CHUNK)

    def pair_copy(way, piece):
        return pltpu.make_async_remote_copy(
            src_ref=part.at[rows_of((1 - core) * 2 + way, piece), :],
            dst_ref=pair_buf.at[way, piece_of(piece), :],
            send_sem=pair_send.at[way, piece],
            recv_sem=pair_recv.at[way, piece],
            device_id=(segment, partner),
            device_id_type=MESH,
        )

    def place(way):
        return chip if way == 1 else last - chip

    def beyond(way):
        ahead = jnp.minimum(chip + 1, last) if way == 1 else jnp.maximum(chip - 1, 0)
        return (segment, ahead * 2 + core)

    def line_copy(way, piece):
        return pltpu.make_async_remote_copy(
            src_ref=line_out.at[way, piece_of(piece), :],
            dst_ref=line_buf.at[way, piece_of(piece), :],
            send_sem=line_send.at[way, piece],
            recv_sem=line_recv.at[way, piece],
            device_id=beyond(way),
            device_id_type=MESH,
        )

    def shift_copy(way, piece):
        entry = jnp.where(turn_out == 1, way, 1 - way)
        return pltpu.make_async_remote_copy(
            src_ref=d_input.at[piece_of(piece), :],
            dst_ref=landed.at[rows_of(core * 2 + way, piece), :],
            send_sem=shift_send.at[piece],
            recv_sem=ring_recv.at[entry, piece],
            device_id=at_target,
            device_id_type=MESH,
        )

    def ring_block(way):
        return jnp.where(turn_in == 1, way, 1 - way)

    def ring_copy(way, piece):
        rows = landed.at[rows_of(core * 2 + ring_block(way), piece), :]
        return pltpu.make_async_remote_copy(
            src_ref=rows,
            dst_ref=rows,
            send_sem=ring_send.at[way, piece],
            recv_sem=ring_recv.at[way, piece],
            device_id=beyond(way),
            device_id_type=MESH,
        )

    def fan_copy(way, piece):
        rows = landed.at[rows_of(core * 2 + ring_block(way), piece), :]
        return pltpu.make_async_remote_copy(
            src_ref=rows,
            dst_ref=rows,
            send_sem=fan_send.at[way, piece],
            recv_sem=fan_recv.at[way, piece],
            device_id=(segment, partner),
            device_id_type=MESH,
        )

    def fan_arrival(way, piece):
        rows = landed.at[rows_of((1 - core) * 2 + ring_block(way), piece), :]
        return pltpu.make_async_remote_copy(
            src_ref=rows,
            dst_ref=rows,
            send_sem=fan_send.at[way, piece],
            recv_sem=fan_recv.at[way, piece],
            device_id=(segment, partner),
            device_id_type=MESH,
        )

    def out_copy(side, way, piece):
        owner = core if side == 0 else 1 - core
        rows = rows_of(owner * 2 + ring_block(way), piece)
        return pltpu.make_async_copy(
            landed.at[rows, :], received.at[rows, :], out_sem.at[side, way, piece]
        )

    def gain_copy(slot, other):
        return pltpu.make_async_remote_copy(
            src_ref=gain_sum,
            dst_ref=gain_buf.at[slot],
            send_sem=gain_send.at[other - 1],
            recv_sem=gain_recv.at[slot],
            device_id=(segment, (member + other) % members),
            device_id_type=MESH,
        )

    def start_pairs(piece, carry):
        for way in range(2):
            pair_copy(way, piece).start()
        return carry

    side = 2 * quarter
    theirs = pl.ds(pl.multiple_of((1 - core) * side, side), side)
    ours = pl.ds(pl.multiple_of(core * side, side), side)
    part[theirs, :] = dot_nt(d_all[theirs, :], w_v[...]).astype(BF16)
    pl.semaphore_wait(barrier, members + 1)
    lax.fori_loop(0, chunks, start_pairs, 0)
    part[ours, :] = dot_nt(d_all[ours, :], w_v[...]).astype(BF16)

    @pl.when(is_end)
    def _():
        gain_sum[...] = jnp.zeros_like(gain_sum)

        def norm_rows(i, carry):
            at = piece_of(i)
            value = x_v[rows_of(owned, i), :].astype(F32)
            centred = value - jnp.mean(value, -1, keepdims=True)
            inv = lax.rsqrt(jnp.mean(centred * centred, -1, keepdims=True) + 1e-05)
            standard[at, :] = centred * inv
            spread[at, :] = jnp.broadcast_to(inv, (CHUNK, 128))
            return carry

        lax.fori_loop(0, chunks, norm_rows, 0)

    def reduce_step(way, piece):
        spot = place(way)
        at = piece_of(piece)
        pair_copy(way, piece).wait_recv()
        total = (
            part[rows_of(core * 2 + way, piece), :].astype(F32)
            + pair_buf[way, at, :].astype(F32)
        )

        @pl.when(spot == 0)
        def _():
            line_out[way, at, :] = total.astype(BF16)
            line_copy(way, piece).start()

        @pl.when(jnp.logical_and(spot > 0, spot < last))
        def _():
            line_copy(way, piece).wait_recv()
            line_out[way, at, :] = (total + line_buf[way, at, :].astype(F32)).astype(BF16)
            line_copy(way, piece).start()

        @pl.when(spot == last)
        def _():
            line_copy(way, piece).wait_recv()
            d_normed = total + line_buf[way, at, :].astype(F32)
            unit = standard[at, :]
            scaled = d_normed * gain_ref[...]
            first_mean = jnp.mean(scaled, -1, keepdims=True)
            second_mean = jnp.mean(scaled * unit, -1, keepdims=True)
            inv = spread[at, :][:, :1]
            d_input[at, :] = (
                g_v[rows_of(owned, piece), :].astype(F32) + inv * (scaled - first_mean - unit * second_mean)
            ).astype(BF16)
            shift_copy(way, piece).start()
            gain_sum[...] += jnp.sum(d_normed * unit, 0, keepdims=True)

            @pl.when(piece == chunks - 1)
            def _():
                slot = jnp.where(chip == last, 2, 0) + core
                for other in range(1, members):
                    gain_copy(slot, other).start()

    def gather_step(way, piece):
        ring_copy(way, piece).wait_recv()

        @pl.when(place(way) < last)
        def _():
            ring_copy(way, piece).start()

        fan_copy(way, piece).start()
        out_copy(0, way, piece).start()

    steps = chunks + LAG * (2 * last + 1)

    wide_pieces = width // BLK
    tall_pieces = (cols + units) // BLK
    grad_start = jnp.where(is_end, GRAD_AT_END, GRAD_AT_MIDDLE)

    def grad_step(piece):
        @pl.when(jnp.logical_and(piece >= 0, piece < wide_pieces))
        def _():
            at = pl.ds(pl.multiple_of(piece * BLK, BLK), BLK)
            value = dot_tn(normed[:, at], d_all[...]).astype(BF16)
            for i in range(3):
                grad_qkv[0, i, at, :] = value[:, i * cols : (i + 1) * cols]
            grad_up[0, at, :] = value[:, 3 * cols :]

        @pl.when(piece == wide_pieces)
        def _():
            grad_out[...] = dot_tn(hidden[:, :cols], g_v[...]).astype(BF16)

        @pl.when(jnp.logical_and(piece > wide_pieces, piece < wide_pieces + tall_pieces))
        def _():
            spot = piece - wide_pieces
            at = pl.ds(pl.multiple_of(spot * BLK, BLK), BLK)
            down_at = pl.ds(pl.multiple_of(spot * BLK - cols, BLK), BLK)
            grad_down[down_at, :] = dot_tn(hidden[:, at], g_v[...]).astype(BF16)

    def slot(k, carry):
        for way in range(2):
            piece = k - LAG * place(way)

            @pl.when(jnp.logical_and(piece >= 0, piece < chunks))
            def _():
                reduce_step(way, piece)

        for way in range(2):
            piece = k - LAG * (last + 1 + place(way))

            @pl.when(jnp.logical_and(piece >= 0, piece < chunks))
            def _():
                gather_step(way, piece)

        grad_step(k - grad_start)
        return carry

    lax.fori_loop(0, steps, slot, 0)

    def finish(piece, carry):
        for way in range(2):
            fan_arrival(way, piece).wait_recv()
            out_copy(1, way, piece).start()
        return carry

    lax.fori_loop(0, chunks, finish, 0)

    owners = (0, 1, members - 2, members - 1)
    total = jnp.zeros_like(gain_sum[...])
    for slot_index, owner in enumerate(owners):

        @pl.when(member != owner)
        def _():
            gain_copy(slot_index, 1).wait_recv()

        @pl.when(member == owner)
        def _():
            gain_buf[slot_index] = gain_sum[...]

        total = total + gain_buf[slot_index]
    gain_out[...] = total

    def settle(piece, carry):
        for way in range(2):
            pair_copy(way, piece).wait_send()
            fan_copy(way, piece).wait_send()
            out_copy(0, way, piece).wait()
            out_copy(1, way, piece).wait()

            @pl.when(place(way) < last)
            def _():
                line_copy(way, piece).wait_send()
                ring_copy(way, piece).wait_send()

            @pl.when(place(way) == last)
            def _():
                shift_copy(way, piece).wait_send()

        return carry

    lax.fori_loop(0, chunks, settle, 0)

    @pl.when(is_end)
    def _():
        for other in range(1, members):
            gain_copy(0, other).wait_send()


def section(sections, members, x, g, gain, qkv, out, up, down, scale, near, valid, patch):
    tokens, width = x.shape
    cols = out.shape[1]
    units = down.shape[1]
    wide = 3 * cols + units
    tall = cols + units
    quarter = tokens // 4
    chunks = quarter // CHUNK
    vmem = pl.BlockSpec(memory_space=pltpu.VMEM)
    hbm = pl.BlockSpec(memory_space=pltpu.HBM)
    shape = jax.ShapeDtypeStruct
    dma = pltpu.SemaphoreType.DMA
    return pl.pallas_call(
        functools.partial(section_kernel, sections, members),
        out_shape=(
            shape((tokens, width), BF16),
            shape((1, width), F32),
            shape((1, 2), F32),
            shape(qkv.shape, BF16),
            shape((cols, width), BF16),
            shape(up.shape, BF16),
            shape((units, width), BF16),
        ),
        in_specs=[hbm] * 11,
        out_specs=[vmem] * 7,
        scratch_shapes=[
            pltpu.VMEM((tokens, width), BF16),
            pltpu.VMEM((tokens, width), BF16),
            pltpu.VMEM((width, wide), BF16),
            pltpu.VMEM((tall, width), BF16),
            pltpu.VMEM((tokens, width), BF16),
            pltpu.VMEM((tokens, wide), F32),
            pltpu.VMEM((tokens, tall), F32),
            pltpu.VMEM((2, tokens, cols), BF16),
            pltpu.VMEM((tokens, cols), BF16),
            pltpu.VMEM((tokens, cols), BF16),
            pltpu.VMEM((2, tokens, cols), BF16),
            pltpu.VMEM((2, tokens, tokens), F32),
            pltpu.VMEM((2, tokens, tokens), F32),
            pltpu.VMEM((2 * tokens, tokens), BF16),
            pltpu.VMEM((2 * tokens, tokens), BF16),
            pltpu.VMEM((2, cols, 2 * tokens), BF16),
            pltpu.VMEM((tokens // BLK, 8, tokens), F32),
            pltpu.VMEM((tokens, tall), BF16),
            pltpu.VMEM((tokens, wide), BF16),
            pltpu.VMEM((tokens, width), BF16),
            pltpu.VMEM((2, quarter, width), BF16),
            pltpu.VMEM((2, quarter, width), BF16),
            pltpu.VMEM((2, quarter, width), BF16),
            pltpu.VMEM((quarter, width), BF16),
            pltpu.VMEM((quarter, width), F32),
            pltpu.VMEM((quarter, 128), F32),
            pltpu.VMEM((tokens, width), BF16),
            pltpu.VMEM((1, width), F32),
            pltpu.VMEM((4, 1, width), F32),
            pltpu.SMEM(patch.shape, jnp.int32),
            pltpu.SMEM((4, 4, near.shape[0]), jnp.int32),
            pltpu.SMEM((4, 4, near.shape[0]), jnp.int32),
            pltpu.SMEM((1, 2), F32),
            pltpu.VMEM((1, width), F32),
            dma((13,)),
            dma((2, chunks)),
            dma((2, chunks)),
            dma((2, chunks)),
            dma((2, chunks)),
            dma((chunks,)),
            dma((2, chunks)),
            dma((2, chunks)),
            dma((2, chunks)),
            dma((2, chunks)),
            dma((members - 1,)),
            dma((4,)),
            dma((2, 2, chunks)),
        ],
        compiler_params=pltpu.CompilerParams(
            collective_id=0, has_side_effects=True, vmem_limit_bytes=48 * 1024 * 1024
        ),
        name="section",
    )(
        patch,
        near.transpose(1, 2, 0),
        valid.transpose(1, 2, 0),
        scale,
        gain,
        x,
        g,
        qkv,
        out[0],
        up,
        down[0],
    )


def place_kernel(*refs):
    count = (len(refs) - 1) // 2
    sems = refs[-1]
    refs[count - 1 + count][...] = refs[count - 1][...]
    copies = [
        pltpu.make_async_copy(refs[i], refs[count + i], sems.at[i]) for i in range(count - 1)
    ]
    for copy in copies:
        copy.start()
    for copy in copies:
        copy.wait()


def placed_results(*arrays):
    vmem = pl.BlockSpec(memory_space=pltpu.VMEM)
    hbm = pl.BlockSpec(memory_space=pltpu.HBM)
    count = len(arrays)
    return pl.pallas_call(
        place_kernel,
        out_shape=tuple(jax.ShapeDtypeStruct(a.shape, a.dtype) for a in arrays),
        in_specs=[vmem] * count,
        out_specs=[hbm] * (count - 1) + [vmem],
        scratch_shapes=[pltpu.SemaphoreType.DMA((count - 1,))],
        compiler_params=pltpu.CompilerParams(vmem_limit_bytes=16 * 1024 * 1024),
        name="placed_results",
    )(*arrays)


def shards(sections, members, *arrays):
    received, gain_grad, grad_scale, grad_qkv, grad_out, grad_up, grad_down = section(
        sections, members, *arrays
    )
    received, grad_qkv, grad_out, grad_up, grad_down, gain_grad, grad_scale = placed_results(
        received, grad_qkv, grad_out, grad_up, grad_down, gain_grad, grad_scale
    )
    return (
        received,
        grad_qkv,
        grad_out[None],
        grad_up,
        grad_down[None],
        gain_grad,
        grad_scale,
    )


def solution(mesh):
    placed = (
        P("segment", None),
        P("segment", None),
        P("segment", None),
        P("segment", None, None, "tp"),
        P("segment", "tp", None),
        P("segment", None, "tp"),
        P("segment", "tp", None),
        P("segment", "tp"),
        P(),
        P(),
        P("segment"),
    )
    return jax.shard_map(
        functools.partial(shards, mesh.shape["segment"], mesh.shape["tp"]),
        mesh=mesh,
        in_specs=placed,
        out_specs=(
            P("segment", None),
            P("segment", None, None, "tp"),
            P("segment", "tp", None),
            P("segment", None, "tp"),
            P("segment", "tp", None),
            P("segment", None),
            P("segment", "tp"),
        ),
        check_vma=False,
    )
```
